32 devices in a mesh: groups: 2 (over x), tracks: 8 (over z, y), frames: 2 (over core).
Axes of the slice: x: 2, y: 2, z: 4, core: 2. Of those that a mesh axis runs over, the one named last changes fastest.
Arguments:
- tokens: bfloat16 [256, 256, 384], P(('groups', 'tracks'), 'frames'), parts along dimension 0, may hold values from -6 to 6
- first_frame: int32 [256], P(('groups', 'tracks')), parts along dimension 0, may hold values from 0 to 127
- visible: int32 [256, 256], P(('groups', 'tracks')), parts along dimension 0, may hold values 0 or 1
- time_qkv: bfloat16 [384, 1152], replicated, may hold values from -0.3125 to 0.3125
- time_output: bfloat16 [384, 384], replicated, may hold values from -0.3125 to 0.3125
- expand: bfloat16 [384, 1536], replicated, may hold values from -0.3125 to 0.3125
- shrink: bfloat16 [1536, 384], replicated, may hold values from -0.15625 to 0.15625
- virtual_init: bfloat16 [64, 384], replicated, may hold values from -6 to 6
- cross_query: bfloat16 [384, 384], replicated, may hold values from -0.3125 to 0.3125
- cross_kv: bfloat16 [384, 768], replicated, may hold values from -0.3125 to 0.3125
- cross_output: bfloat16 [384, 384], replicated, may hold values from -1.25 to 1.25
- self_qkv: bfloat16 [384, 1152], replicated, may hold values from -0.3125 to 0.3125
- self_output: bfloat16 [384, 384], replicated, may hold values from -0.625 to 0.625
- back_query: bfloat16 [384, 384], replicated, may hold values from -0.3125 to 0.3125
- back_kv: bfloat16 [384, 768], replicated, may hold values from -0.3125 to 0.3125
- back_output: bfloat16 [384, 384], replicated, may hold values from -1.25 to 1.25
Outputs:
- tracked: bfloat16 [256, 256, 384], P(('groups', 'tracks'), 'frames'), parts along dimension 0
The draws below stay inside these ranges and needn't reach their ends.
There are 2 independent parts, one for each index of `groups`. The reference program is written for one: setup_inputs(seed, part) draws one part's arguments, and reference() takes and returns one part's arrays. A program takes and returns all parts, laid end to end along the dimension named above; an argument that names none is the same for every part. Nothing has to cross between parts.
Inputs may be any that keep to these rules, and one draw needn't show every extreme that they name: `first_frame`: each track's first frame.
All inputs are finite; a program needn't handle non-finite values. No bound on the sum of `visible` on one device may be relied on, other than what follows from the above.
Results may differ from the reference program's by a relative error of at most 0.0095.
Values may be sent and summed in bfloat16 or wider, within the bound.
A program may use at most 128 MiB of HBM per device.

```python
import jax
import jax.numpy as jnp
from jax import lax

D = 384
FF = 1536
HEADS = 8
VIRT = 64
HEAD = 48
TRK_DEV = 16
FRM_DEV = 128
TRACKS = 128
FRAMES = 256
N_TRACKS = 8
N_FRAMES = 2


def touch_ends(drawn, rng, smallest, high):
    spot = [jax.random.randint(jax.random.fold_in(rng, axis), (), 0, length) for axis, length in enumerate(drawn.shape)]
    main_axis = drawn.shape.index(max(drawn.shape))
    next_to = spot[:main_axis] + [(spot[main_axis] + 1) % drawn.shape[main_axis]] + spot[main_axis + 1:]
    return drawn.at[tuple(spot)].set(smallest).at[tuple(next_to)].set(high)


def steps_of(stream_key, shape, cuts, smallest, high):
    def one(dim, shards_of):
        steps = jax.random.uniform(jax.random.fold_in(jax.random.fold_in(stream_key, 6), dim), (shards_of,), jnp.float32, smallest / len(cuts), high / len(cuts))
        return jnp.repeat(jnp.exp(steps), shape[dim] // shards_of).reshape((-1,) + (1,) * (len(shape) - dim - 1))

    level = one(*cuts[0])
    for cut in cuts[1:]:
        level = level * one(*cut)
    return level


def gaussian(stream_key, dims, width, most, cuts=(), kind=jnp.bfloat16):
    factor_of = steps_of(stream_key, dims, cuts, -0.22, 0.18) if cuts else 1.0
    array = jax.random.normal(stream_key, dims, jnp.float32) * width * factor_of
    return jnp.minimum(jnp.maximum(array, -most), most).astype(kind)


def setup_inputs(seed: int = 0, part: int = 0) -> dict:
    keys = jax.random.split(jax.random.key(seed), 17)
    own_keys = jax.random.split(jax.random.fold_in(keys[16], part), 17)
    tokens = gaussian(own_keys[0], (TRACKS, FRAMES, D), 1.0, 6.0, ((0, 8), (1, 2)))
    first_frame = touch_ends(jax.random.randint(own_keys[1], (TRACKS,), 0, FRAMES // 2), jax.random.fold_in(own_keys[1], 1), 0, (FRAMES // 2) - 1).astype(jnp.int32)
    visible = touch_ends((jax.random.randint(own_keys[2], (TRACKS, FRAMES), 0, 4) < 3).astype(jnp.int32), jax.random.fold_in(own_keys[2], 1), 0, 1)
    time_qkv = gaussian(keys[3], (D, 3 * D), D ** -0.5, 0.3125)
    time_output = gaussian(keys[4], (D, D), D ** -0.5, 0.3125)
    expand = gaussian(keys[5], (D, FF), D ** -0.5, 0.3125)
    shrink = gaussian(keys[6], (FF, D), FF ** -0.5, 0.15625)
    virtual_init = gaussian(keys[7], (VIRT, D), 1.0, 6.0)
    cross_query = gaussian(keys[8], (D, D), D ** -0.5, 0.3125)
    cross_kv = gaussian(keys[9], (D, 2 * D), D ** -0.5, 0.3125)
    cross_output = gaussian(keys[10], (D, D), (D // 16) ** -0.5, 1.25)
    self_qkv = gaussian(keys[11], (D, 3 * D), D ** -0.5, 0.3125)
    self_output = gaussian(keys[12], (D, D), (D // 4) ** -0.5, 0.625)
    back_query = gaussian(keys[13], (D, D), D ** -0.5, 0.3125)
    back_kv = gaussian(keys[14], (D, 2 * D), D ** -0.5, 0.3125)
    back_output = gaussian(keys[15], (D, D), (D // 16) ** -0.5, 1.25)
    return {"tokens": tokens, "first_frame": first_frame, "visible": visible, "time_qkv": time_qkv, "time_output": time_output, "expand": expand, "shrink": shrink, "virtual_init": virtual_init, "cross_query": cross_query, "cross_kv": cross_kv, "cross_output": cross_output, "self_qkv": self_qkv, "self_output": self_output, "back_query": back_query, "back_kv": back_kv, "back_output": back_output}


def normed(values):
    values = values.astype(jnp.float32)
    return values * lax.rsqrt(lax.optimization_barrier(jnp.mean(values * values, axis=-1, keepdims=True)) + 1e-06)

def product(pattern, first_operand, second_operand):
    return jnp.einsum(pattern, first_operand.astype(jnp.float32), second_operand.astype(jnp.float32))

def split_heads(values):
    return values.reshape(values.shape[:-1] + (HEADS, HEAD))

def merge_heads(values):
    return values.reshape(values.shape[:-2] + (D,))

def usable_keys(first_frame, visible, offset, length):
    frames = offset + jnp.arange(length, dtype=jnp.int32)
    seen = lax.dynamic_slice_in_dim(visible, offset, length, 1)
    return (frames[None, :] >= first_frame[:, None]) & ((seen == 1) | (frames[None, :] == first_frame[:, None]))

def time_project(tokens, time_qkv):
    projected = product('ntd,dk->ntk', normed(tokens).astype(jnp.bfloat16), time_qkv)
    time_query = normed(projected[..., :D]).astype(jnp.bfloat16)
    time_key = normed(projected[..., D:2 * D]).astype(jnp.bfloat16)
    time_value = projected[..., 2 * D:].astype(jnp.bfloat16)
    return (time_query, time_key, time_value)

def time_terms(time_query, key_piece, value_piece, usable):
    scores = product('nqhe,nkhe->nhqk', split_heads(time_query), split_heads(key_piece)) * HEAD ** (-0.5)
    weights = (jnp.exp(scores) * usable[:, None, None, :].astype(jnp.float32)).astype(jnp.bfloat16)
    numerator = product('nhqk,nkhe->nqhe', weights, split_heads(value_piece))
    denominator = jnp.transpose(lax.optimization_barrier(jnp.sum(weights.astype(jnp.float32), axis=-1)), (0, 2, 1))
    return (numerator, denominator)

def time_finish(tokens, numerator, denominator, time_output, expand, shrink):
    time_mixed = merge_heads(numerator / denominator[..., None]).astype(jnp.bfloat16)
    middle = tokens.astype(jnp.float32) + product('ntd,dk->ntk', time_mixed, time_output)
    middle_norm = normed(middle).astype(jnp.bfloat16)
    hidden = jax.nn.gelu(product('ntd,df->ntf', middle_norm, expand), approximate=True).astype(jnp.bfloat16)
    return (middle + product('ntf,fd->ntd', hidden, shrink)).astype(jnp.bfloat16)

def attend_pair(query, key, value, query_form, value_form):
    weights = jnp.exp(product(query_form, split_heads(query), split_heads(key)) * HEAD ** (-0.5)).astype(jnp.bfloat16)
    numerator = product(value_form, weights, split_heads(value))
    return (weights, numerator)

def virtual_block(settled, virtual_init, cross_query, cross_kv, cross_output, self_qkv, self_output, back_query, back_kv, back_output):
    settled_norm = normed(settled).astype(jnp.bfloat16)
    crossed = product('nfd,dk->nfk', settled_norm, cross_kv)
    track_key = normed(crossed[..., :D]).astype(jnp.bfloat16)
    track_value = crossed[..., D:].astype(jnp.bfloat16)
    virtual_norm = normed(virtual_init).astype(jnp.bfloat16)
    virtual_query = normed(product('jd,dk->jk', virtual_norm, cross_query)).astype(jnp.bfloat16)
    cross_weight, numerator = attend_pair(virtual_query, track_key, track_value, 'jhe,nfhe->fhjn', 'fhjn,nfhe->fjhe')
    totals = jnp.transpose(lax.optimization_barrier(jnp.sum(cross_weight.astype(jnp.float32), axis=-1)), (0, 2, 1))
    cross_mixed = merge_heads(numerator / totals[..., None]).astype(jnp.bfloat16)
    virtual_first = virtual_init.astype(jnp.float32)[None] + product('fjd,dk->fjk', cross_mixed, cross_output)
    selfed = product('fjd,dk->fjk', normed(virtual_first).astype(jnp.bfloat16), self_qkv)
    self_query = normed(selfed[..., :D]).astype(jnp.bfloat16)
    self_key = normed(selfed[..., D:2 * D]).astype(jnp.bfloat16)
    self_value = selfed[..., 2 * D:].astype(jnp.bfloat16)
    self_weight, numerator = attend_pair(self_query, self_key, self_value, 'fjhe,fihe->fhji', 'fhji,fihe->fjhe')
    totals = jnp.transpose(lax.optimization_barrier(jnp.sum(self_weight.astype(jnp.float32), axis=-1)), (0, 2, 1))
    self_mixed = merge_heads(numerator / totals[..., None]).astype(jnp.bfloat16)
    virtual_second = virtual_first + product('fjd,dk->fjk', self_mixed, self_output)
    backed = product('fjd,dk->fjk', normed(virtual_second).astype(jnp.bfloat16), back_kv)
    virtual_key = normed(backed[..., :D]).astype(jnp.bfloat16)
    virtual_value = backed[..., D:].astype(jnp.bfloat16)
    track_query = normed(product('nfd,dk->nfk', settled_norm, back_query)).astype(jnp.bfloat16)
    back_weight, numerator = attend_pair(track_query, virtual_key, virtual_value, 'nfhe,fjhe->nfhj', 'nfhj,fjhe->nfhe')
    totals = lax.optimization_barrier(jnp.sum(back_weight.astype(jnp.float32), axis=-1))
    back_mixed = merge_heads(numerator / totals[..., None]).astype(jnp.bfloat16)
    return (settled.astype(jnp.float32) + product('nfd,dk->nfk', back_mixed, back_output)).astype(jnp.bfloat16)

def reference(tokens, first_frame, visible, time_qkv, time_output, expand, shrink, virtual_init, cross_query, cross_kv, cross_output, self_qkv, self_output, back_query, back_kv, back_output):
    track_block = TRK_DEV // N_FRAMES
    blocks = TRACKS // track_block

    def time_part(grouped):
        time_query, time_key, time_value = time_project(grouped[0], time_qkv)
        usable = usable_keys(grouped[1], grouped[2], 0, FRAMES)
        numerator, denominator = time_terms(time_query, time_key, time_value, usable)
        return time_finish(grouped[0], numerator, denominator, time_output, expand, shrink)
    settled = lax.map(time_part, (tokens.reshape(blocks, track_block, FRAMES, D), first_frame.reshape(blocks, track_block), visible.reshape(blocks, track_block, FRAMES)))
    settled = settled.reshape(TRACKS, FRAMES, D)
    frame_block = FRM_DEV // N_TRACKS
    pieces = jnp.transpose(settled.reshape(TRACKS, FRAMES // frame_block, frame_block, D), (1, 0, 2, 3))

    def virtual_part(section):
        return virtual_block(section, virtual_init, cross_query, cross_kv, cross_output, self_qkv, self_output, back_query, back_kv, back_output)
    tracked = lax.map(virtual_part, pieces)
    return jnp.transpose(tracked, (1, 0, 2, 3)).reshape(TRACKS, FRAMES, D)
```

```python
import functools

import jax
import jax.numpy as jnp
from jax import lax
from jax.experimental import pallas as pl
from jax.experimental.pallas import tpu as pltpu
from jax.sharding import PartitionSpec as P

D = 384
HEADS = 8
HEAD = 48


def normed(values):
    values = values.astype(jnp.float32)
    return values * lax.rsqrt(jnp.mean(values * values, axis=-1, keepdims=True) + 1e-06)


def product(pattern, first_operand, second_operand):
    return jnp.einsum(pattern, first_operand, second_operand, preferred_element_type=jnp.float32)


def split_heads(values):
    return values.reshape(values.shape[:-1] + (HEADS, HEAD))


def merge_heads(values):
    return values.reshape(values.shape[:-2] + (D,))


def usable_keys(first_frame, visible, length):
    frames = jnp.arange(length, dtype=jnp.int32)
    return (frames[None, :] >= first_frame[:, None]) & (
        (visible == 1) | (frames[None, :] == first_frame[:, None])
    )


def time_project(tokens, time_qkv):
    projected = product("ntd,dk->ntk", normed(tokens).astype(jnp.bfloat16), time_qkv)
    time_query = normed(projected[..., :D]).astype(jnp.bfloat16)
    time_key = normed(projected[..., D : 2 * D]).astype(jnp.bfloat16)
    time_value = projected[..., 2 * D :].astype(jnp.bfloat16)
    return (time_query, time_key, time_value)


def time_terms(time_query, key_piece, value_piece, usable):
    scores = product("nqhe,nkhe->nhqk", split_heads(time_query), split_heads(key_piece)) * HEAD ** (
        -0.5
    )
    weights = (jnp.exp(scores) * usable[:, None, None, :].astype(jnp.float32)).astype(jnp.bfloat16)
    numerator = product("nhqk,nkhe->nqhe", weights, split_heads(value_piece))
    denominator = jnp.transpose(jnp.sum(weights.astype(jnp.float32), axis=-1), (0, 2, 1))
    return (numerator, denominator)


def time_finish(tokens, numerator, denominator, time_output, expand, shrink):
    time_mixed = merge_heads(numerator / denominator[..., None]).astype(jnp.bfloat16)
    middle = tokens.astype(jnp.float32) + product("ntd,dk->ntk", time_mixed, time_output)
    middle_norm = normed(middle).astype(jnp.bfloat16)
    hidden = jax.nn.gelu(product("ntd,df->ntf", middle_norm, expand), approximate=True).astype(
        jnp.bfloat16
    )
    return (middle + product("ntf,fd->ntd", hidden, shrink)).astype(jnp.bfloat16)


def track_complete(whole, first_frame, visible, time_qkv, time_output, expand, shrink):
    half_tracks = whole.shape[0]
    core_index = lax.axis_index("frames")
    own_first = lax.dynamic_slice_in_dim(first_frame, core_index * half_tracks, half_tracks, 0)
    own_visible = lax.dynamic_slice_in_dim(visible, core_index * half_tracks, half_tracks, 0)
    time_query, time_key, time_value = time_project(whole, time_qkv)
    usable = usable_keys(own_first, own_visible, whole.shape[1])
    numerator, denominator = time_terms(time_query, time_key, time_value, usable)
    return time_finish(whole, numerator, denominator, time_output, expand, shrink)


def attend_pair(query, key, value, query_form, value_form):
    weights = jnp.exp(
        product(query_form, split_heads(query), split_heads(key)) * HEAD ** (-0.5)
    ).astype(jnp.bfloat16)
    numerator = product(value_form, weights, split_heads(value))
    return (weights, numerator)


def virtual_block(
    settled,
    virtual_init,
    cross_query,
    cross_kv,
    cross_output,
    self_qkv,
    self_output,
    back_query,
    back_kv,
    back_output,
):
    settled_norm = normed(settled).astype(jnp.bfloat16)
    crossed = product("nfd,dk->nfk", settled_norm, cross_kv)
    track_key = normed(crossed[..., :D]).astype(jnp.bfloat16)
    track_value = crossed[..., D:].astype(jnp.bfloat16)
    virtual_norm = normed(virtual_init).astype(jnp.bfloat16)
    virtual_query = normed(product("jd,dk->jk", virtual_norm, cross_query)).astype(jnp.bfloat16)
    cross_weight, numerator = attend_pair(
        virtual_query, track_key, track_value, "jhe,nfhe->fhjn", "fhjn,nfhe->fjhe"
    )
    totals = jnp.transpose(jnp.sum(cross_weight.astype(jnp.float32), axis=-1), (0, 2, 1))
    cross_mixed = merge_heads(numerator / totals[..., None]).astype(jnp.bfloat16)
    virtual_first = virtual_init.astype(jnp.float32)[None] + product(
        "fjd,dk->fjk", cross_mixed, cross_output
    )
    selfed = product("fjd,dk->fjk", normed(virtual_first).astype(jnp.bfloat16), self_qkv)
    self_query = normed(selfed[..., :D]).astype(jnp.bfloat16)
    self_key = normed(selfed[..., D : 2 * D]).astype(jnp.bfloat16)
    self_value = selfed[..., 2 * D :].astype(jnp.bfloat16)
    self_weight, numerator = attend_pair(
        self_query, self_key, self_value, "fjhe,fihe->fhji", "fhji,fihe->fjhe"
    )
    totals = jnp.transpose(jnp.sum(self_weight.astype(jnp.float32), axis=-1), (0, 2, 1))
    self_mixed = merge_heads(numerator / totals[..., None]).astype(jnp.bfloat16)
    virtual_second = virtual_first + product("fjd,dk->fjk", self_mixed, self_output)
    backed = product("fjd,dk->fjk", normed(virtual_second).astype(jnp.bfloat16), back_kv)
    virtual_key = normed(backed[..., :D]).astype(jnp.bfloat16)
    virtual_value = backed[..., D:].astype(jnp.bfloat16)
    track_query = normed(product("nfd,dk->nfk", settled_norm, back_query)).astype(jnp.bfloat16)
    back_weight, numerator = attend_pair(
        track_query, virtual_key, virtual_value, "nfhe,fjhe->nfhj", "nfhj,fjhe->nfhe"
    )
    totals = jnp.sum(back_weight.astype(jnp.float32), axis=-1)
    back_mixed = merge_heads(numerator / totals[..., None]).astype(jnp.bfloat16)
    return (settled.astype(jnp.float32) + product("nfd,dk->nfk", back_mixed, back_output)).astype(
        jnp.bfloat16
    )


def per_device(
    tokens,
    first_frame,
    visible,
    time_qkv,
    time_output,
    expand,
    shrink,
    virtual_init,
    cross_query,
    cross_kv,
    cross_output,
    self_qkv,
    self_output,
    back_query,
    back_kv,
    back_output,
):
    whole = lax.all_to_all(tokens, "frames", split_axis=0, concat_axis=1, tiled=True)
    settled = track_complete(whole, first_frame, visible, time_qkv, time_output, expand, shrink)
    spread = lax.all_to_all(settled, ("tracks", "frames"), split_axis=1, concat_axis=0, tiled=True)
    joined = lax.all_to_all(
        virtual_block(
            spread,
            virtual_init,
            cross_query,
            cross_kv,
            cross_output,
            self_qkv,
            self_output,
            back_query,
            back_kv,
            back_output,
        ),
        ("tracks", "frames"),
        split_axis=0,
        concat_axis=1,
        tiled=True,
    )
    tracked = lax.all_to_all(joined, "frames", split_axis=1, concat_axis=0, tiled=True)
    return tracked


def row_scale(values):
    return lax.rsqrt(jnp.mean(values * values, axis=-1, keepdims=True) + 1e-06)


def unit(values):
    return values * row_scale(values)


def dot(first, second):
    return jnp.dot(first, second, preferred_element_type=jnp.float32)


def dot_t(first, second):
    return lax.dot_general(
        first, second, (((1,), (1,)), ((), ())), preferred_element_type=jnp.float32
    )


WIN = 256
GROUP = HEADS // 2
USED = GROUP * HEAD
SHIFT = D - WIN
STARTS = (0, SHIFT)
BASES = (0, USED - SHIFT)
SPARE = (USED, 0)
LOG2E = 1.4426950408889634
QSCALE = HEAD ** (-0.5) * LOG2E


def head_mask(group, head, rows):
    lane = lax.broadcasted_iota(jnp.int32, (rows, WIN), 1)
    low = BASES[group] + head * HEAD
    return (lane >= low) & (lane < low + HEAD)


def window(values, group):
    return values[:, STARTS[group] : STARTS[group] + WIN]


def with_ones(values, group):
    part = window(values, group)
    lane = lax.broadcasted_iota(jnp.int32, part.shape, 1)
    inside = (lane >= BASES[group]) & (lane < BASES[group] + USED)
    return jnp.where(inside, part, jnp.ones_like(part))


def join_windows(first, second):
    return jnp.concatenate(
        [first[:, :SHIFT], first[:, SHIFT:] + second[:, :SHIFT], second[:, SHIFT:]], axis=1
    )


def picked(summed, group, head):
    share = 1.0 / summed[:, SPARE[group] : SPARE[group] + 1]
    return jnp.where(head_mask(group, head, summed.shape[0]), summed * share, 0.0)


def head_stack(values, group):
    part = window(values, group)
    return jnp.concatenate(
        [
            jnp.where(head_mask(group, h, part.shape[0]), part, jnp.zeros_like(part))
            for h in range(GROUP)
        ],
        axis=0,
    )


def time_keys(key, value, usable):
    held = []
    for group in range(2):
        values = (with_ones(value, group) * usable).astype(jnp.bfloat16)
        held.append((window(key, group), values))
    return held


def time_attend(query, held):
    halves = []
    for group, (keys, values) in enumerate(held):
        queries = window(query, group)
        total = None
        for head in range(GROUP):
            mask = head_mask(group, head, queries.shape[0])
            own = jnp.where(mask, queries, jnp.zeros_like(queries))
            weights = jnp.exp2(dot_t(own, keys)).astype(jnp.bfloat16)
            part = picked(dot(weights, values), group, head)
            total = part if total is None else total + part
        halves.append(total)
    return join_windows(*halves)


def time_queries(x, w_qkv):
    projected = dot(unit(x).astype(jnp.bfloat16), w_qkv[...])
    query = (unit(projected[:, :D]) * QSCALE).astype(jnp.bfloat16)
    key = unit(projected[:, D : 2 * D]).astype(jnp.bfloat16)
    return query, key, projected[:, 2 * D :]


def time_close(x, mixed, w_out, w_expand, w_shrink):
    middle = x + dot(mixed.astype(jnp.bfloat16), w_out[...])
    inner = dot(unit(middle).astype(jnp.bfloat16), w_expand[...])
    half = 0.5 * inner
    bent = jnp.tanh(inner * (0.7978845608028654 + 0.035677408136300125 * (inner * inner)))
    hidden = (half + half * bent).astype(jnp.bfloat16)
    return middle + dot(hidden, w_shrink[...])


def stacked_attention(queries, keys, values, ones_stack):
    nums, dens = [], []
    for group in range(2):
        weights = jnp.exp2(dot_t(window(queries, group), head_stack(keys, group))).astype(
            jnp.bfloat16
        )
        nums.append(dot(weights, head_stack(values, group)))
        dens.append(dot(weights, ones_stack[group]))
    return join_windows(*nums) / join_windows(*dens)


def frame_rows(s, query_stack, ones_stack, virtual, frames, refs):
    w_ckv, w_cout, w_sqkv, w_sout, w_bq, w_bkv, w_bout = refs
    tracks = s.shape[0] // frames
    virt = virtual.shape[0]
    sf = s.astype(jnp.float32)
    sn = unit(sf).astype(jnp.bfloat16)
    crossed = dot(sn, w_ckv[...])
    track_key = unit(crossed[:, :D]).astype(jnp.bfloat16)
    track_value = crossed[:, D:].astype(jnp.bfloat16)
    track_query = (unit(dot(sn, w_bq[...])) * QSCALE).astype(jnp.bfloat16)
    mixed = []
    for i in range(frames):
        rows = slice(i * tracks, (i + 1) * tracks)
        halves = []
        for group in range(2):
            weights = jnp.exp2(
                dot_t(query_stack[group], window(track_key[rows], group))
            ).astype(jnp.bfloat16)
            summed = dot(weights, with_ones(track_value[rows], group))
            total = None
            for head in range(GROUP):
                part = picked(summed[head * virt : (head + 1) * virt], group, head)
                total = part if total is None else total + part
            halves.append(total)
        mixed.append(join_windows(*halves))
    mixed = jnp.concatenate(mixed, axis=0).astype(jnp.bfloat16)
    first = jnp.concatenate([virtual] * frames, axis=0) + dot(mixed, w_cout[...])
    selfed = dot(unit(first).astype(jnp.bfloat16), w_sqkv[...])
    self_query = (unit(selfed[:, :D]) * QSCALE).astype(jnp.bfloat16)
    self_key = unit(selfed[:, D : 2 * D]).astype(jnp.bfloat16)
    self_value = selfed[:, 2 * D :].astype(jnp.bfloat16)
    mixed = []
    for i in range(frames):
        rows = slice(i * virt, (i + 1) * virt)
        mixed.append(
            stacked_attention(self_query[rows], self_key[rows], self_value[rows], ones_stack)
        )
    mixed = jnp.concatenate(mixed, axis=0).astype(jnp.bfloat16)
    second = first + dot(mixed, w_sout[...])
    backed = dot(unit(second).astype(jnp.bfloat16), w_bkv[...])
    virtual_key = unit(backed[:, :D]).astype(jnp.bfloat16)
    virtual_value = backed[:, D:].astype(jnp.bfloat16)
    mixed = []
    for i in range(frames):
        rows = slice(i * tracks, (i + 1) * tracks)
        cols = slice(i * virt, (i + 1) * virt)
        mixed.append(
            stacked_attention(track_query[rows], virtual_key[cols], virtual_value[cols], ones_stack)
        )
    mixed = jnp.concatenate(mixed, axis=0).astype(jnp.bfloat16)
    return (sf + dot(mixed, w_bout[...])).astype(jnp.bfloat16)


STEP_FRAMES = 4
SINGLE_TRACKS = 2
STEP_TRACKS = 2
EARLY_PAIRS = 0
OCTET = 8
VMEM_BYTES = 62 * 1024 * 1024
MESH = pl.DeviceIdType.MESH
OUT = pltpu.VMEM


def turn_matrix(side, mine, cores, own_frames):
    pairs = (mine - SINGLE_TRACKS) // STEP_TRACKS
    single_rows = cores * SINGLE_TRACKS * own_frames
    pair_rows = cores * pairs * STEP_TRACKS * OCTET
    tracks = cores * mine
    shape = (OCTET * tracks, single_rows + pair_rows)
    row = lax.broadcasted_iota(jnp.int32, shape, 0)
    col = lax.broadcasted_iota(jnp.int32, shape, 1)
    frame, track = row // tracks, row % tracks
    core, n = track // mine, track % mine
    single = (core * SINGLE_TRACKS + n) * own_frames + side * OCTET + frame
    late = n - SINGLE_TRACKS
    pair = single_rows + (core * pairs + late // STEP_TRACKS) * (STEP_TRACKS * OCTET)
    pair = pair + (late % STEP_TRACKS) * OCTET + frame
    source = jnp.where(late < 0, single, pair)
    return jnp.where(col == source, 1.0, 0.0).astype(jnp.bfloat16)


def partner(me, count, k):
    half = count // 2
    inner = lax.rem((me * 4 // count + 1) // 2, 2)
    step = inner * k + (1 - inner) * (count - 2 - k)
    turn = step // half
    side = lax.rem(me // half + 1 + turn, 2)
    return side * half + lax.rem(lax.rem(me, half) + lax.rem(step, half) + turn, half)


def layer_kernel(n_tracks_axis, n_frames_axis, n_weights, *refs):
    tokens, first_frame, visible, virtual_init = refs[:4]
    stored = refs[4 : 4 + n_weights]
    returned = refs[4 + n_weights]
    loaded = refs[5 + n_weights : 5 + 2 * n_weights]
    (
        own,
        other,
        settled_one,
        settled_two,
        spread_one,
        spread_two,
        by_frame,
        result,
        query_stack,
        ones_stack,
        usable,
        swap,
        weight_sem,
        own_sem,
        pair_send,
        pair_recv,
        spread_send,
        spread_recv,
        back_send,
        back_recv,
    ) = refs[5 + 2 * n_weights :]
    w_qkv, w_out, w_expand, w_shrink, w_cq = loaded[:5]
    late = loaded[5:]
    t = lax.axis_index("tracks")
    f = lax.axis_index("frames")
    group_index = lax.axis_index("groups")
    devices = n_tracks_axis * n_frames_axis
    me = t * n_frames_axis + f
    held, part, _ = tokens.shape
    mine = held // n_frames_axis
    length = part * n_frames_axis
    own_frames = length // devices
    all_tracks = held * n_tracks_axis
    virt = virtual_init.shape[0]
    pairs = (mine - SINGLE_TRACKS) // STEP_TRACKS
    late_pairs = pairs - EARLY_PAIRS
    blocks = own_frames // OCTET

    def place(index):
        return (group_index, index // n_frames_axis, index % n_frames_axis)

    barrier = pltpu.get_barrier_semaphore()

    @pl.loop(1, devices)
    def _(k):
        pl.semaphore_signal(
            barrier,
            inc=1,
            device_id=place(lax.rem(me + k, devices)),
            device_id_type=MESH,
        )

    def own_copy(n):
        return pltpu.make_async_copy(tokens.at[f * mine + n], own.at[n], own_sem.at[n])

    loads = [
        pltpu.make_async_copy(stored[k], loaded[k], weight_sem.at[k]) for k in range(n_weights)
    ]
    own_copy(0).start()
    for load in loads[:4]:
        load.start()

    @pl.loop(1, mine)
    def _(n):
        own_copy(n).start()

    for load in loads[4:]:
        load.start()

    usable[...] = jnp.transpose(visible[...].astype(jnp.float32), (1, 0))
    for side in range(blocks):
        swap[side] = turn_matrix(side, mine, n_frames_axis, own_frames)
    for group in range(2):
        ones_stack[group] = jnp.concatenate(
            [
                jnp.where(head_mask(group, h, virt), 1.0, 0.0).astype(jnp.bfloat16)
                for h in range(GROUP)
            ],
            axis=0,
        )

    pl.semaphore_wait(barrier, devices - 1)

    def pair_copy(n):
        return pltpu.make_async_remote_copy(
            src_ref=tokens.at[(1 - f) * mine + n],
            dst_ref=other.at[n],
            send_sem=pair_send.at[n],
            recv_sem=pair_recv.at[n],
            device_id=(group_index, t, 1 - f),
            device_id_type=MESH,
        )

    @pl.loop(0, mine)
    def _(n):
        pair_copy(n).start()

    def send(src, dst, sem, index):
        pltpu.make_async_remote_copy(
            src_ref=src,
            dst_ref=dst,
            send_sem=spread_send,
            recv_sem=spread_recv.at[sem],
            device_id=place(index),
            device_id_type=MESH,
        ).start()

    def base_of(index):
        return lax.rem(index + f, n_frames_axis) * part + (index // n_frames_axis) * own_frames

    def send_single(n, side):
        dst = spread_one.at[me, n]

        def source(index):
            at = pl.multiple_of(base_of(index), own_frames)
            return settled_one.at[n, pl.ds(at, own_frames), :]

        core = lax.rem(f + side, n_frames_axis)

        @pl.loop(0, n_tracks_axis - 1)
        def _(k):
            index = partner(t, n_tracks_axis, k) * n_frames_axis + core
            send(source(index), dst, 0, index)

        if side == 0:
            pltpu.make_async_copy(source(me), dst, spread_recv.at[0]).start()
        else:
            index = t * n_frames_axis + core
            send(source(index), dst, 0, index)

    def send_pairs(p, count, block, n_blocks, sem):
        if n_blocks == blocks:
            dst = spread_two.at[me, p]
        else:
            dst = spread_two.at[me, pl.ds(p, count), block]

        def source(index):
            at = base_of(index) // OCTET + block
            if n_blocks == blocks:
                return settled_two.at[p, pl.ds(at, blocks)]
            return settled_two.at[pl.ds(p, count), at]

        @pl.loop(0, devices - 1)
        def _(k):
            index = partner(me, devices, k)
            send(source(index), dst, sem, index)

        pltpu.make_async_copy(source(me), dst, spread_recv.at[sem]).start()

    lane = lax.broadcasted_iota(jnp.int32, (part, held), 1)

    def gather(n):
        own_copy(n).wait()
        pair_copy(n).wait_recv()
        chosen = lane == f * mine + n
        started = first_frame[f * mine + n]
        column = []
        for side in range(n_frames_axis):
            at = pl.multiple_of(lax.rem(f + side, n_frames_axis) * part, part)
            seen = jnp.where(chosen, usable[pl.ds(at, part), :], 0.0)
            seen = jnp.sum(seen, axis=1, keepdims=True)
            ids = at + lax.broadcasted_iota(jnp.int32, (part, 1), 0)
            kept = (ids >= started) & ((seen == 1.0) | (ids == started))
            column.append(jnp.where(kept, 1.0, 0.0))
        return [own[n], other[n]], jnp.concatenate(column, axis=0)

    for load in loads[:4]:
        load.wait()

    @pl.loop(0, SINGLE_TRACKS)
    def _(n):
        pieces, flags = gather(n)
        x = jnp.concatenate(pieces, axis=0).astype(jnp.float32)
        query, key, value = time_queries(x, w_qkv)
        mixed = time_attend(query, time_keys(key, value, flags))
        done = time_close(x, mixed, w_out, w_expand, w_shrink)
        settled_one[n] = done.astype(jnp.bfloat16)
        for side in range(n_frames_axis):
            send_single(n, side)

    @pl.loop(0, pairs)
    def _(p):
        pieces, flags = [], []
        for k in range(STEP_TRACKS):
            piece, flag = gather(SINGLE_TRACKS + p * STEP_TRACKS + k)
            pieces += piece
            flags.append(flag)
        x = jnp.concatenate(pieces, axis=0).astype(jnp.float32)
        query, key, value = time_queries(x, w_qkv)
        mixed = []
        for k in range(STEP_TRACKS):
            rows = slice(k * length, (k + 1) * length)
            mixed.append(time_attend(query[rows], time_keys(key[rows], value[rows], flags[k])))
        done = time_close(x, jnp.concatenate(mixed, axis=0), w_out, w_expand, w_shrink)
        done = done.reshape(STEP_TRACKS, length // OCTET, OCTET, D)
        done = jnp.transpose(done, (1, 0, 2, 3)).reshape(length // OCTET, STEP_TRACKS * OCTET, D)
        settled_two[p] = done.astype(jnp.bfloat16)

        if EARLY_PAIRS:

            @pl.when(p < EARLY_PAIRS)
            def _():
                send_pairs(p, 1, 0, blocks, 1)

        @pl.when(p >= EARLY_PAIRS)
        def _():
            send_pairs(p, 1, 0, 1, 2)

    for block in range(1, blocks):
        send_pairs(EARLY_PAIRS, late_pairs, block, 1, 2 + block)

    for load in loads[4:]:
        load.wait()
    virtual = virtual_init[...].astype(jnp.float32)
    virtual_query = unit(dot(unit(virtual).astype(jnp.bfloat16), w_cq[...])) * QSCALE
    for group in range(2):
        query_stack[group] = head_stack(virtual_query, group).astype(jnp.bfloat16)

    @pl.loop(0, mine)
    def _(n):
        pair_copy(n).wait_send()

    def arrived(ref, sem):
        pltpu.make_async_copy(ref, ref, spread_recv.at[sem]).wait()

    arrived(spread_one, 0)
    if EARLY_PAIRS:
        arrived(spread_two.at[:, pl.ds(0, EARLY_PAIRS)], 1)

    @pl.loop(0, blocks)
    def _(side):
        arrived(spread_two.at[:, pl.ds(EARLY_PAIRS, late_pairs), 0], 2 + side)
        at_frame = pl.multiple_of(side * OCTET, OCTET)

        @pl.loop(0, n_tracks_axis)
        def _(c):
            one = spread_one[pl.ds(c * n_frames_axis, n_frames_axis)]
            two = spread_two[pl.ds(c * n_frames_axis, n_frames_axis), :, side]
            rows = jnp.concatenate([one.reshape(-1, D), two.reshape(-1, D)], axis=0)
            turned = dot(swap[side], rows).astype(jnp.bfloat16)
            at = pl.multiple_of(c * held, held)
            by_frame[pl.ds(at_frame, OCTET), pl.ds(at, held), :] = turned.reshape(OCTET, held, D)

        @pl.loop(0, OCTET // STEP_FRAMES)
        def _(step):
            f0 = side * OCTET + step * STEP_FRAMES
            s = by_frame[pl.ds(f0, STEP_FRAMES)].reshape(STEP_FRAMES * all_tracks, D)
            done = frame_rows(
                s,
                query_stack,
                ones_stack,
                virtual_init[...].astype(jnp.float32),
                STEP_FRAMES,
                late,
            )
            result[pl.ds(f0, STEP_FRAMES)] = done.reshape(STEP_FRAMES, all_tracks, D)
            dst = returned.at[t, pl.ds(f0, STEP_FRAMES)]

            def source(index):
                return result.at[
                    pl.ds(f0, STEP_FRAMES), pl.ds(pl.multiple_of(index * held, held), held), :
                ]

            @pl.loop(0, n_tracks_axis - 1)
            def _(k):
                index = partner(t, n_tracks_axis, k)
                pltpu.make_async_remote_copy(
                    src_ref=source(index),
                    dst_ref=dst,
                    send_sem=back_send,
                    recv_sem=back_recv,
                    device_id=(group_index, index, f),
                    device_id_type=MESH,
                ).start()

            pltpu.make_async_copy(source(t), dst, back_recv).start()

    others = length - own_frames
    sent = settled_one.at[:, pl.ds(0, others), :]
    pltpu.make_async_copy(sent, sent, spread_send).wait()
    sent = settled_two.at[:, pl.ds(0, others // OCTET)]
    pltpu.make_async_copy(sent, sent, spread_send).wait()
    sent = result.at[:, pl.ds(0, all_tracks - held), :]
    pltpu.make_async_copy(sent, sent, back_send).wait()
    pltpu.make_async_copy(returned, returned, back_recv).wait()


def fused_device(n_tracks_axis, n_frames_axis, tokens, first_frame, visible, *rest):
    (w_qkv, w_out, w_expand, w_shrink, virtual_init, w_cq, *late) = rest
    weights = (w_qkv, w_out, w_expand, w_shrink, w_cq, *late)
    held, part, _ = tokens.shape
    mine = held // n_frames_axis
    length = part * n_frames_axis
    devices = n_tracks_axis * n_frames_axis
    own_frames = length // devices
    all_tracks = held * n_tracks_axis
    pairs = (mine - SINGLE_TRACKS) // STEP_TRACKS
    unit_rows = STEP_TRACKS * OCTET
    blocks = own_frames // OCTET
    vmem = pl.BlockSpec(memory_space=pltpu.VMEM)
    hbm = pl.BlockSpec(memory_space=pltpu.HBM)
    virt = virtual_init.shape[0]
    bf16 = jnp.bfloat16
    dma = pltpu.SemaphoreType.DMA
    turn_rows = n_frames_axis * (SINGLE_TRACKS * own_frames + pairs * unit_rows)
    returned = pl.pallas_call(
        functools.partial(layer_kernel, n_tracks_axis, n_frames_axis, len(weights)),
        out_shape=OUT((n_tracks_axis, own_frames, held, D), bf16),
        in_specs=[hbm, pl.BlockSpec(memory_space=pltpu.SMEM), vmem, vmem] + [hbm] * len(weights),
        out_specs=pl.BlockSpec(memory_space=OUT),
        scratch_shapes=[pltpu.VMEM(w.shape, w.dtype) for w in weights]
        + [
            pltpu.VMEM((mine, part, D), bf16),
            pltpu.VMEM((mine, part, D), bf16),
            pltpu.VMEM((SINGLE_TRACKS, length, D), bf16),
            pltpu.VMEM((pairs, length // OCTET, unit_rows, D), bf16),
            pltpu.VMEM((devices, SINGLE_TRACKS, own_frames, D), bf16),
            pltpu.VMEM((devices, pairs, blocks, unit_rows, D), bf16),
            pltpu.VMEM((own_frames, all_tracks, D), bf16),
            pltpu.VMEM((own_frames, all_tracks, D), bf16),
            pltpu.VMEM((2, GROUP * virt, WIN), bf16),
            pltpu.VMEM((2, GROUP * virt, WIN), bf16),
            pltpu.VMEM((length, held), jnp.float32),
            pltpu.VMEM((blocks, OCTET * held, turn_rows), bf16),
            dma((len(weights),)),
            dma((mine,)),
            dma((mine,)),
            dma((mine,)),
            dma,
            dma((2 + blocks,)),
            dma,
            dma,
        ],
        compiler_params=pltpu.CompilerParams(
            collective_id=0, has_side_effects=True, vmem_limit_bytes=VMEM_BYTES
        ),
    )(tokens, first_frame, visible, virtual_init, *weights)
    return jnp.transpose(returned, (2, 0, 1, 3)).reshape(tokens.shape)


def fits(tracks_axis, frames_axis, tokens):
    held = tokens.shape[0]
    own_frames = tokens.shape[1] // tracks_axis
    mine = held // 2
    return (
        frames_axis == 2
        and tracks_axis % 2 == 0
        and mine > SINGLE_TRACKS
        and (mine - SINGLE_TRACKS) % STEP_TRACKS == 0
        and own_frames == held
        and own_frames == 2 * OCTET
        and STEP_TRACKS * OCTET == 16
        and tokens.shape[1] % 128 == 0
    )


def solution(mesh):
    placed = (
        P(("groups", "tracks"), "frames", None),
        P(("groups", "tracks")),
        P(("groups", "tracks"), None),
        P(),
        P(),
        P(),
        P(),
        P(),
        P(),
        P(),
        P(),
        P(),
        P(),
        P(),
        P(),
        P(),
    )
    axes = (mesh.shape["tracks"], mesh.shape["frames"])

    def body(tokens, *rest):
        if fits(*axes, tokens):
            return fused_device(*axes, tokens, *rest)
        return per_device(tokens, *rest)

    return jax.shard_map(
        body,
        mesh=mesh,
        in_specs=placed,
        out_specs=P(("groups", "tracks"), "frames", None),
        check_vma=False,
    )
```

```python
import functools

import jax
import jax.numpy as jnp
from jax import lax
from jax.experimental import pallas as pl
from jax.experimental.pallas import tpu as pltpu
from jax.sharding import PartitionSpec as P

D = 384
HEADS = 8
HEAD = 48


def normed(values):
    values = values.astype(jnp.float32)
    return values * lax.rsqrt(jnp.mean(values * values, axis=-1, keepdims=True) + 1e-06)


def product(pattern, first_operand, second_operand):
    return jnp.einsum(pattern, first_operand, second_operand, preferred_element_type=jnp.float32)


def split_heads(values):
    return values.reshape(values.shape[:-1] + (HEADS, HEAD))


def merge_heads(values):
    return values.reshape(values.shape[:-2] + (D,))


def usable_keys(first_frame, visible, length):
    frames = jnp.arange(length, dtype=jnp.int32)
    return (frames[None, :] >= first_frame[:, None]) & (
        (visible == 1) | (frames[None, :] == first_frame[:, None])
    )


def time_project(tokens, time_qkv):
    projected = product("ntd,dk->ntk", normed(tokens).astype(jnp.bfloat16), time_qkv)
    time_query = normed(projected[..., :D]).astype(jnp.bfloat16)
    time_key = normed(projected[..., D : 2 * D]).astype(jnp.bfloat16)
    time_value = projected[..., 2 * D :].astype(jnp.bfloat16)
    return (time_query, time_key, time_value)


def time_terms(time_query, key_piece, value_piece, usable):
    scores = product("nqhe,nkhe->nhqk", split_heads(time_query), split_heads(key_piece)) * HEAD ** (
        -0.5
    )
    weights = (jnp.exp(scores) * usable[:, None, None, :].astype(jnp.float32)).astype(jnp.bfloat16)
    numerator = product("nhqk,nkhe->nqhe", weights, split_heads(value_piece))
    denominator = jnp.transpose(jnp.sum(weights.astype(jnp.float32), axis=-1), (0, 2, 1))
    return (numerator, denominator)


def time_finish(tokens, numerator, denominator, time_output, expand, shrink):
    time_mixed = merge_heads(numerator / denominator[..., None]).astype(jnp.bfloat16)
    middle = tokens.astype(jnp.float32) + product("ntd,dk->ntk", time_mixed, time_output)
    middle_norm = normed(middle).astype(jnp.bfloat16)
    hidden = jax.nn.gelu(product("ntd,df->ntf", middle_norm, expand), approximate=True).astype(
        jnp.bfloat16
    )
    return (middle + product("ntf,fd->ntd", hidden, shrink)).astype(jnp.bfloat16)


def track_complete(whole, first_frame, visible, time_qkv, time_output, expand, shrink):
    half_tracks = whole.shape[0]
    core_index = lax.axis_index("frames")
    own_first = lax.dynamic_slice_in_dim(first_frame, core_index * half_tracks, half_tracks, 0)
    own_visible = lax.dynamic_slice_in_dim(visible, core_index * half_tracks, half_tracks, 0)
    time_query, time_key, time_value = time_project(whole, time_qkv)
    usable = usable_keys(own_first, own_visible, whole.shape[1])
    numerator, denominator = time_terms(time_query, time_key, time_value, usable)
    return time_finish(whole, numerator, denominator, time_output, expand, shrink)


def attend_pair(query, key, value, query_form, value_form):
    weights = jnp.exp(
        product(query_form, split_heads(query), split_heads(key)) * HEAD ** (-0.5)
    ).astype(jnp.bfloat16)
    numerator = product(value_form, weights, split_heads(value))
    return (weights, numerator)


def virtual_block(
    settled,
    virtual_init,
    cross_query,
    cross_kv,
    cross_output,
    self_qkv,
    self_output,
    back_query,
    back_kv,
    back_output,
):
    settled_norm = normed(settled).astype(jnp.bfloat16)
    crossed = product("nfd,dk->nfk", settled_norm, cross_kv)
    track_key = normed(crossed[..., :D]).astype(jnp.bfloat16)
    track_value = crossed[..., D:].astype(jnp.bfloat16)
    virtual_norm = normed(virtual_init).astype(jnp.bfloat16)
    virtual_query = normed(product("jd,dk->jk", virtual_norm, cross_query)).astype(jnp.bfloat16)
    cross_weight, numerator = attend_pair(
        virtual_query, track_key, track_value, "jhe,nfhe->fhjn", "fhjn,nfhe->fjhe"
    )
    totals = jnp.transpose(jnp.sum(cross_weight.astype(jnp.float32), axis=-1), (0, 2, 1))
    cross_mixed = merge_heads(numerator / totals[..., None]).astype(jnp.bfloat16)
    virtual_first = virtual_init.astype(jnp.float32)[None] + product(
        "fjd,dk->fjk", cross_mixed, cross_output
    )
    selfed = product("fjd,dk->fjk", normed(virtual_first).astype(jnp.bfloat16), self_qkv)
    self_query = normed(selfed[..., :D]).astype(jnp.bfloat16)
    self_key = normed(selfed[..., D : 2 * D]).astype(jnp.bfloat16)
    self_value = selfed[..., 2 * D :].astype(jnp.bfloat16)
    self_weight, numerator = attend_pair(
        self_query, self_key, self_value, "fjhe,fihe->fhji", "fhji,fihe->fjhe"
    )
    totals = jnp.transpose(jnp.sum(self_weight.astype(jnp.float32), axis=-1), (0, 2, 1))
    self_mixed = merge_heads(numerator / totals[..., None]).astype(jnp.bfloat16)
    virtual_second = virtual_first + product("fjd,dk->fjk", self_mixed, self_output)
    backed = product("fjd,dk->fjk", normed(virtual_second).astype(jnp.bfloat16), back_kv)
    virtual_key = normed(backed[..., :D]).astype(jnp.bfloat16)
    virtual_value = backed[..., D:].astype(jnp.bfloat16)
    track_query = normed(product("nfd,dk->nfk", settled_norm, back_query)).astype(jnp.bfloat16)
    back_weight, numerator = attend_pair(
        track_query, virtual_key, virtual_value, "nfhe,fjhe->nfhj", "nfhj,fjhe->nfhe"
    )
    totals = jnp.sum(back_weight.astype(jnp.float32), axis=-1)
    back_mixed = merge_heads(numerator / totals[..., None]).astype(jnp.bfloat16)
    return (settled.astype(jnp.float32) + product("nfd,dk->nfk", back_mixed, back_output)).astype(
        jnp.bfloat16
    )


def per_device(
    tokens,
    first_frame,
    visible,
    time_qkv,
    time_output,
    expand,
    shrink,
    virtual_init,
    cross_query,
    cross_kv,
    cross_output,
    self_qkv,
    self_output,
    back_query,
    back_kv,
    back_output,
):
    whole = lax.all_to_all(tokens, "frames", split_axis=0, concat_axis=1, tiled=True)
    settled = track_complete(whole, first_frame, visible, time_qkv, time_output, expand, shrink)
    spread = lax.all_to_all(settled, ("tracks", "frames"), split_axis=1, concat_axis=0, tiled=True)
    joined = lax.all_to_all(
        virtual_block(
            spread,
            virtual_init,
            cross_query,
            cross_kv,
            cross_output,
            self_qkv,
            self_output,
            back_query,
            back_kv,
            back_output,
        ),
        ("tracks", "frames"),
        split_axis=0,
        concat_axis=1,
        tiled=True,
    )
    tracked = lax.all_to_all(joined, "frames", split_axis=1, concat_axis=0, tiled=True)
    return tracked


def row_scale(values):
    return lax.rsqrt(jnp.mean(values * values, axis=-1, keepdims=True) + 1e-06)


def unit(values):
    return values * row_scale(values)


def dot(first, second):
    return jnp.dot(first, second, preferred_element_type=jnp.float32)


def dot_t(first, second):
    return lax.dot_general(
        first, second, (((1,), (1,)), ((), ())), preferred_element_type=jnp.float32
    )


WIN = 256
GROUP = HEADS // 2
USED = GROUP * HEAD
SHIFT = D - WIN
STARTS = (0, SHIFT)
BASES = (0, USED - SHIFT)
SPARE = (USED, 0)
LOG2E = 1.4426950408889634
QSCALE = HEAD ** (-0.5) * LOG2E


def head_mask(group, head, rows):
    lane = lax.broadcasted_iota(jnp.int32, (rows, WIN), 1)
    low = BASES[group] + head * HEAD
    return (lane >= low) & (lane < low + HEAD)


def window(values, group):
    return values[:, STARTS[group] : STARTS[group] + WIN]


def with_ones(values, group):
    part = window(values, group)
    lane = lax.broadcasted_iota(jnp.int32, part.shape, 1)
    inside = (lane >= BASES[group]) & (lane < BASES[group] + USED)
    return jnp.where(inside, part, jnp.ones_like(part))


def join_windows(first, second):
    return jnp.concatenate(
        [first[:, :SHIFT], first[:, SHIFT:] + second[:, :SHIFT], second[:, SHIFT:]], axis=1
    )


def picked(summed, group, head):
    share = 1.0 / summed[:, SPARE[group] : SPARE[group] + 1]
    return jnp.where(head_mask(group, head, summed.shape[0]), summed * share, 0.0)


def head_stack(values, group):
    part = window(values, group)
    return jnp.concatenate(
        [
            jnp.where(head_mask(group, h, part.shape[0]), part, jnp.zeros_like(part))
            for h in range(GROUP)
        ],
        axis=0,
    )


def time_keys(key, value, usable):
    held = []
    for group in range(2):
        values = (with_ones(value, group) * usable).astype(jnp.bfloat16)
        held.append((window(key, group), values))
    return held


def time_attend(query, held):
    halves = []
    for group, (keys, values) in enumerate(held):
        queries = window(query, group)
        total = None
        for head in range(GROUP):
            mask = head_mask(group, head, queries.shape[0])
            own = jnp.where(mask, queries, jnp.zeros_like(queries))
            weights = jnp.exp2(dot_t(own, keys)).astype(jnp.bfloat16)
            part = picked(dot(weights, values), group, head)
            total = part if total is None else total + part
        halves.append(total)
    return join_windows(*halves)


def time_queries(x, w_qkv):
    projected = dot(unit(x).astype(jnp.bfloat16), w_qkv[...])
    query = (unit(projected[:, :D]) * QSCALE).astype(jnp.bfloat16)
    key = unit(projected[:, D : 2 * D]).astype(jnp.bfloat16)
    return query, key, projected[:, 2 * D :]


def time_close(x, mixed, w_out, w_expand, w_shrink):
    middle = x + dot(mixed.astype(jnp.bfloat16), w_out[...])
    inner = dot(unit(middle).astype(jnp.bfloat16), w_expand[...])
    half = 0.5 * inner
    bent = jnp.tanh(inner * (0.7978845608028654 + 0.035677408136300125 * (inner * inner)))
    hidden = (half + half * bent).astype(jnp.bfloat16)
    return middle + dot(hidden, w_shrink[...])


def stacked_attention(queries, keys, values, ones_stack):
    nums, dens = [], []
    for group in range(2):
        weights = jnp.exp2(dot_t(window(queries, group), head_stack(keys, group))).astype(
            jnp.bfloat16
        )
        nums.append(dot(weights, head_stack(values, group)))
        dens.append(dot(weights, ones_stack[group]))
    return join_windows(*nums) / join_windows(*dens)


def frame_rows(s, query_stack, ones_stack, virtual, frames, refs):
    w_ckv, w_cout, w_sqkv, w_sout, w_bq, w_bkv, w_bout = refs
    tracks = s.shape[0] // frames
    virt = virtual.shape[0]
    sf = s.astype(jnp.float32)
    sn = unit(sf).astype(jnp.bfloat16)
    crossed = dot(sn, w_ckv[...])
    track_key = unit(crossed[:, :D]).astype(jnp.bfloat16)
    track_value = crossed[:, D:].astype(jnp.bfloat16)
    track_query = (unit(dot(sn, w_bq[...])) * QSCALE).astype(jnp.bfloat16)
    mixed = []
    for i in range(frames):
        rows = slice(i * tracks, (i + 1) * tracks)
        halves = []
        for group in range(2):
            weights = jnp.exp2(
                dot_t(query_stack[group], window(track_key[rows], group))
            ).astype(jnp.bfloat16)
            summed = dot(weights, with_ones(track_value[rows], group))
            total = None
            for head in range(GROUP):
                part = picked(summed[head * virt : (head + 1) * virt], group, head)
                total = part if total is None else total + part
            halves.append(total)
        mixed.append(join_windows(*halves))
    mixed = jnp.concatenate(mixed, axis=0).astype(jnp.bfloat16)
    first = jnp.concatenate([virtual] * frames, axis=0) + dot(mixed, w_cout[...])
    selfed = dot(unit(first).astype(jnp.bfloat16), w_sqkv[...])
    self_query = (unit(selfed[:, :D]) * QSCALE).astype(jnp.bfloat16)
    self_key = unit(selfed[:, D : 2 * D]).astype(jnp.bfloat16)
    self_value = selfed[:, 2 * D :].astype(jnp.bfloat16)
    mixed = []
    for i in range(frames):
        rows = slice(i * virt, (i + 1) * virt)
        mixed.append(
            stacked_attention(self_query[rows], self_key[rows], self_value[rows], ones_stack)
        )
    mixed = jnp.concatenate(mixed, axis=0).astype(jnp.bfloat16)
    second = first + dot(mixed, w_sout[...])
    backed = dot(unit(second).astype(jnp.bfloat16), w_bkv[...])
    virtual_key = unit(backed[:, :D]).astype(jnp.bfloat16)
    virtual_value = backed[:, D:].astype(jnp.bfloat16)
    mixed = []
    for i in range(frames):
        rows = slice(i * tracks, (i + 1) * tracks)
        cols = slice(i * virt, (i + 1) * virt)
        mixed.append(
            stacked_attention(track_query[rows], virtual_key[cols], virtual_value[cols], ones_stack)
        )
    mixed = jnp.concatenate(mixed, axis=0).astype(jnp.bfloat16)
    return (sf + dot(mixed, w_bout[...])).astype(jnp.bfloat16)


STEP_FRAMES = 4
SINGLE_TRACKS = 2
STEP_TRACKS = 2
EARLY_PAIRS = 0
OCTET = 8
VMEM_BYTES = 62 * 1024 * 1024
MESH = pl.DeviceIdType.MESH
OUT = pltpu.VMEM


def turn_matrix(side, mine, cores, own_frames):
    pairs = (mine - SINGLE_TRACKS) // STEP_TRACKS
    single_rows = cores * SINGLE_TRACKS * own_frames
    pair_rows = cores * pairs * STEP_TRACKS * OCTET
    tracks = cores * mine
    shape = (OCTET * tracks, single_rows + pair_rows)
    row = lax.broadcasted_iota(jnp.int32, shape, 0)
    col = lax.broadcasted_iota(jnp.int32, shape, 1)
    frame, track = row // tracks, row % tracks
    core, n = track // mine, track % mine
    single = (core * SINGLE_TRACKS + n) * own_frames + side * OCTET + frame
    late = n - SINGLE_TRACKS
    pair = single_rows + (core * pairs + late // STEP_TRACKS) * (STEP_TRACKS * OCTET)
    pair = pair + (late % STEP_TRACKS) * OCTET + frame
    source = jnp.where(late < 0, single, pair)
    return jnp.where(col == source, 1.0, 0.0).astype(jnp.bfloat16)


def partner(me, count, k):
    half = count // 2
    inner = lax.rem((me * 4 // count + 1) // 2, 2)
    step = inner * k + (1 - inner) * (count - 2 - k)
    turn = step // half
    side = lax.rem(me // half + 1 + turn, 2)
    return side * half + lax.rem(lax.rem(me, half) + lax.rem(step, half) + turn, half)


def ordered(me, count, k):
    half = count // 2
    side = me // half
    cross = (1 - side) * half + k
    near = side * half + (k - half) + jnp.where(side * half + (k - half) >= me, 1, 0)
    return jnp.where(k < half, cross, near)


def layer_kernel(n_tracks_axis, n_frames_axis, n_weights, *refs):
    tokens, first_frame, visible, virtual_init = refs[:4]
    stored = refs[4 : 4 + n_weights]
    returned = refs[4 + n_weights]
    loaded = refs[5 + n_weights : 5 + 2 * n_weights]
    (
        own,
        other,
        settled_one,
        settled_two,
        spread_one,
        spread_two,
        by_frame,
        result,
        query_stack,
        ones_stack,
        usable,
        swap,
        weight_sem,
        own_sem,
        pair_send,
        pair_recv,
        spread_send,
        spread_recv,
        back_send,
        back_recv,
    ) = refs[5 + 2 * n_weights :]
    w_qkv, w_out, w_expand, w_shrink, w_cq = loaded[:5]
    late = loaded[5:]
    t = lax.axis_index("tracks")
    f = lax.axis_index("frames")
    group_index = lax.axis_index("groups")
    devices = n_tracks_axis * n_frames_axis
    me = t * n_frames_axis + f
    held, part, _ = tokens.shape
    mine = held // n_frames_axis
    length = part * n_frames_axis
    own_frames = length // devices
    all_tracks = held * n_tracks_axis
    virt = virtual_init.shape[0]
    pairs = (mine - SINGLE_TRACKS) // STEP_TRACKS
    late_pairs = pairs - EARLY_PAIRS
    blocks = own_frames // OCTET

    def place(index):
        return (group_index, index // n_frames_axis, index % n_frames_axis)

    barrier = pltpu.get_barrier_semaphore()

    @pl.loop(1, devices)
    def _(k):
        pl.semaphore_signal(
            barrier,
            inc=1,
            device_id=place(lax.rem(me + k, devices)),
            device_id_type=MESH,
        )

    def own_copy(n):
        return pltpu.make_async_copy(tokens.at[f * mine + n], own.at[n], own_sem.at[n])

    loads = [
        pltpu.make_async_copy(stored[k], loaded[k], weight_sem.at[k]) for k in range(n_weights)
    ]
    own_copy(0).start()
    for load in loads[:4]:
        load.start()

    @pl.loop(1, mine)
    def _(n):
        own_copy(n).start()

    for load in loads[4:]:
        load.start()

    usable[...] = jnp.transpose(visible[...].astype(jnp.float32), (1, 0))
    for side in range(blocks):
        swap[side] = turn_matrix(side, mine, n_frames_axis, own_frames)
    for group in range(2):
        ones_stack[group] = jnp.concatenate(
            [
                jnp.where(head_mask(group, h, virt), 1.0, 0.0).astype(jnp.bfloat16)
                for h in range(GROUP)
            ],
            axis=0,
        )

    pl.semaphore_wait(barrier, devices - 1)

    def pair_copy(n):
        return pltpu.make_async_remote_copy(
            src_ref=tokens.at[(1 - f) * mine + n],
            dst_ref=other.at[n],
            send_sem=pair_send.at[n],
            recv_sem=pair_recv.at[n],
            device_id=(group_index, t, 1 - f),
            device_id_type=MESH,
        )

    @pl.loop(0, mine)
    def _(n):
        pair_copy(n).start()

    def send(src, dst, sem, index):
        pltpu.make_async_remote_copy(
            src_ref=src,
            dst_ref=dst,
            send_sem=spread_send,
            recv_sem=spread_recv.at[sem],
            device_id=place(index),
            device_id_type=MESH,
        ).start()

    def base_of(index):
        return lax.rem(index + f, n_frames_axis) * part + (index // n_frames_axis) * own_frames

    def send_single(n, side):
        dst = spread_one.at[me, n]

        def source(index):
            at = pl.multiple_of(base_of(index), own_frames)
            return settled_one.at[n, pl.ds(at, own_frames), :]

        core = lax.rem(f + side, n_frames_axis)

        @pl.loop(0, n_tracks_axis - 1, unroll=True)
        def _(k):
            index = ordered(t, n_tracks_axis, k) * n_frames_axis + core
            send(source(index), dst, 0, index)

        if side == 0:
            pltpu.make_async_copy(source(me), dst, spread_recv.at[0]).start()
        else:
            index = t * n_frames_axis + core
            send(source(index), dst, 0, index)

    def send_pairs(p, count, block, n_blocks, sem):
        if n_blocks == blocks:
            dst = spread_two.at[me, p]
        else:
            dst = spread_two.at[me, pl.ds(p, count), block]

        def source(index):
            at = base_of(index) // OCTET + block
            if n_blocks == blocks:
                return settled_two.at[p, pl.ds(at, blocks)]
            return settled_two.at[pl.ds(p, count), at]

        @pl.loop(0, devices - 1, unroll=True)
        def _(k):
            index = ordered(me, devices, k)
            send(source(index), dst, sem, index)

        pltpu.make_async_copy(source(me), dst, spread_recv.at[sem]).start()

    lane = lax.broadcasted_iota(jnp.int32, (part, held), 1)

    def gather(n):
        own_copy(n).wait()
        pair_copy(n).wait_recv()
        chosen = lane == f * mine + n
        started = first_frame[f * mine + n]
        column = []
        for side in range(n_frames_axis):
            at = pl.multiple_of(lax.rem(f + side, n_frames_axis) * part, part)
            seen = jnp.where(chosen, usable[pl.ds(at, part), :], 0.0)
            seen = jnp.sum(seen, axis=1, keepdims=True)
            ids = at + lax.broadcasted_iota(jnp.int32, (part, 1), 0)
            kept = (ids >= started) & ((seen == 1.0) | (ids == started))
            column.append(jnp.where(kept, 1.0, 0.0))
        return [own[n], other[n]], jnp.concatenate(column, axis=0)

    for load in loads[:4]:
        load.wait()

    @pl.loop(0, SINGLE_TRACKS)
    def _(n):
        pieces, flags = gather(n)
        x = jnp.concatenate(pieces, axis=0).astype(jnp.float32)
        query, key, value = time_queries(x, w_qkv)
        mixed = time_attend(query, time_keys(key, value, flags))
        done = time_close(x, mixed, w_out, w_expand, w_shrink)
        settled_one[n] = done.astype(jnp.bfloat16)
        for side in range(n_frames_axis):
            send_single(n, side)

    @pl.loop(0, pairs)
    def _(p):
        pieces, flags = [], []
        for k in range(STEP_TRACKS):
            piece, flag = gather(SINGLE_TRACKS + p * STEP_TRACKS + k)
            pieces += piece
            flags.append(flag)
        x = jnp.concatenate(pieces, axis=0).astype(jnp.float32)
        query, key, value = time_queries(x, w_qkv)
        mixed = []
        for k in range(STEP_TRACKS):
            rows = slice(k * length, (k + 1) * length)
            mixed.append(time_attend(query[rows], time_keys(key[rows], value[rows], flags[k])))
        done = time_close(x, jnp.concatenate(mixed, axis=0), w_out, w_expand, w_shrink)
        done = done.reshape(STEP_TRACKS, length // OCTET, OCTET, D)
        done = jnp.transpose(done, (1, 0, 2, 3)).reshape(length // OCTET, STEP_TRACKS * OCTET, D)
        settled_two[p] = done.astype(jnp.bfloat16)

        if EARLY_PAIRS:

            @pl.when(p < EARLY_PAIRS)
            def _():
                send_pairs(p, 1, 0, blocks, 1)

        @pl.when(p >= EARLY_PAIRS)
        def _():
            send_pairs(p, 1, 0, 1, 2)

    for block in range(1, blocks):
        send_pairs(EARLY_PAIRS, late_pairs, block, 1, 2 + block)

    for load in loads[4:]:
        load.wait()
    virtual = virtual_init[...].astype(jnp.float32)
    virtual_query = unit(dot(unit(virtual).astype(jnp.bfloat16), w_cq[...])) * QSCALE
    for group in range(2):
        query_stack[group] = head_stack(virtual_query, group).astype(jnp.bfloat16)

    @pl.loop(0, mine)
    def _(n):
        pair_copy(n).wait_send()

    def arrived(ref, sem):
        pltpu.make_async_copy(ref, ref, spread_recv.at[sem]).wait()

    arrived(spread_one, 0)
    if EARLY_PAIRS:
        arrived(spread_two.at[:, pl.ds(0, EARLY_PAIRS)], 1)

    @pl.loop(0, blocks)
    def _(side):
        arrived(spread_two.at[:, pl.ds(EARLY_PAIRS, late_pairs), 0], 2 + side)
        at_frame = pl.multiple_of(side * OCTET, OCTET)

        @pl.loop(0, n_tracks_axis)
        def _(c):
            one = spread_one[pl.ds(c * n_frames_axis, n_frames_axis)]
            two = spread_two[pl.ds(c * n_frames_axis, n_frames_axis), :, side]
            rows = jnp.concatenate([one.reshape(-1, D), two.reshape(-1, D)], axis=0)
            turned = dot(swap[side], rows).astype(jnp.bfloat16)
            at = pl.multiple_of(c * held, held)
            by_frame[pl.ds(at_frame, OCTET), pl.ds(at, held), :] = turned.reshape(OCTET, held, D)

        @pl.loop(0, OCTET // STEP_FRAMES)
        def _(step):
            f0 = side * OCTET + step * STEP_FRAMES
            s = by_frame[pl.ds(f0, STEP_FRAMES)].reshape(STEP_FRAMES * all_tracks, D)
            done = frame_rows(
                s,
                query_stack,
                ones_stack,
                virtual_init[...].astype(jnp.float32),
                STEP_FRAMES,
                late,
            )
            result[pl.ds(f0, STEP_FRAMES)] = done.reshape(STEP_FRAMES, all_tracks, D)
            dst = returned.at[t, pl.ds(f0, STEP_FRAMES)]

            def source(index):
                return result.at[
                    pl.ds(f0, STEP_FRAMES), pl.ds(pl.multiple_of(index * held, held), held), :
                ]

            @pl.loop(0, n_tracks_axis - 1, unroll=True)
            def _(k):
                index = ordered(t, n_tracks_axis, k)
                pltpu.make_async_remote_copy(
                    src_ref=source(index),
                    dst_ref=dst,
                    send_sem=back_send,
                    recv_sem=back_recv,
                    device_id=(group_index, index, f),
                    device_id_type=MESH,
                ).start()

            pltpu.make_async_copy(source(t), dst, back_recv).start()

    others = length - own_frames
    sent = settled_one.at[:, pl.ds(0, others), :]
    pltpu.make_async_copy(sent, sent, spread_send).wait()
    sent = settled_two.at[:, pl.ds(0, others // OCTET)]
    pltpu.make_async_copy(sent, sent, spread_send).wait()
    sent = result.at[:, pl.ds(0, all_tracks - held), :]
    pltpu.make_async_copy(sent, sent, back_send).wait()
    pltpu.make_async_copy(returned, returned, back_recv).wait()


def fused_device(n_tracks_axis, n_frames_axis, tokens, first_frame, visible, *rest):
    (w_qkv, w_out, w_expand, w_shrink, virtual_init, w_cq, *late) = rest
    weights = (w_qkv, w_out, w_expand, w_shrink, w_cq, *late)
    held, part, _ = tokens.shape
    mine = held // n_frames_axis
    length = part * n_frames_axis
    devices = n_tracks_axis * n_frames_axis
    own_frames = length // devices
    all_tracks = held * n_tracks_axis
    pairs = (mine - SINGLE_TRACKS) // STEP_TRACKS
    unit_rows = STEP_TRACKS * OCTET
    blocks = own_frames // OCTET
    vmem = pl.BlockSpec(memory_space=pltpu.VMEM)
    hbm = pl.BlockSpec(memory_space=pltpu.HBM)
    virt = virtual_init.shape[0]
    bf16 = jnp.bfloat16
    dma = pltpu.SemaphoreType.DMA
    turn_rows = n_frames_axis * (SINGLE_TRACKS * own_frames + pairs * unit_rows)
    returned = pl.pallas_call(
        functools.partial(layer_kernel, n_tracks_axis, n_frames_axis, len(weights)),
        out_shape=OUT((n_tracks_axis, own_frames, held, D), bf16),
        in_specs=[hbm, pl.BlockSpec(memory_space=pltpu.SMEM), vmem, vmem] + [hbm] * len(weights),
        out_specs=pl.BlockSpec(memory_space=OUT),
        scratch_shapes=[pltpu.VMEM(w.shape, w.dtype) for w in weights]
        + [
            pltpu.VMEM((mine, part, D), bf16),
            pltpu.VMEM((mine, part, D), bf16),
            pltpu.VMEM((SINGLE_TRACKS, length, D), bf16),
            pltpu.VMEM((pairs, length // OCTET, unit_rows, D), bf16),
            pltpu.VMEM((devices, SINGLE_TRACKS, own_frames, D), bf16),
            pltpu.VMEM((devices, pairs, blocks, unit_rows, D), bf16),
            pltpu.VMEM((own_frames, all_tracks, D), bf16),
            pltpu.VMEM((own_frames, all_tracks, D), bf16),
            pltpu.VMEM((2, GROUP * virt, WIN), bf16),
            pltpu.VMEM((2, GROUP * virt, WIN), bf16),
            pltpu.VMEM((length, held), jnp.float32),
            pltpu.VMEM((blocks, OCTET * held, turn_rows), bf16),
            dma((len(weights),)),
            dma((mine,)),
            dma((mine,)),
            dma((mine,)),
            dma,
            dma((2 + blocks,)),
            dma,
            dma,
        ],
        compiler_params=pltpu.CompilerParams(
            collective_id=0, has_side_effects=True, vmem_limit_bytes=VMEM_BYTES
        ),
    )(tokens, first_frame, visible, virtual_init, *weights)
    return jnp.transpose(returned, (2, 0, 1, 3)).reshape(tokens.shape)


def fits(tracks_axis, frames_axis, tokens):
    held = tokens.shape[0]
    own_frames = tokens.shape[1] // tracks_axis
    mine = held // 2
    return (
        frames_axis == 2
        and tracks_axis % 2 == 0
        and mine > SINGLE_TRACKS
        and (mine - SINGLE_TRACKS) % STEP_TRACKS == 0
        and own_frames == held
        and own_frames == 2 * OCTET
        and STEP_TRACKS * OCTET == 16
        and tokens.shape[1] % 128 == 0
    )


def solution(mesh):
    placed = (
        P(("groups", "tracks"), "frames", None),
        P(("groups", "tracks")),
        P(("groups", "tracks"), None),
        P(),
        P(),
        P(),
        P(),
        P(),
        P(),
        P(),
        P(),
        P(),
        P(),
        P(),
        P(),
        P(),
    )
    axes = (mesh.shape["tracks"], mesh.shape["frames"])

    def body(tokens, *rest):
        if fits(*axes, tokens):
            return fused_device(*axes, tokens, *rest)
        return per_device(tokens, *rest)

    return jax.shard_map(
        body,
        mesh=mesh,
        in_specs=placed,
        out_specs=P(("groups", "tracks"), "frames", None),
        check_vma=False,
    )
```

```python
import functools

import jax
import jax.numpy as jnp
from jax import lax
from jax.experimental import pallas as pl
from jax.experimental.pallas import tpu as pltpu
from jax.sharding import PartitionSpec as P

D = 384
HEADS = 8
HEAD = 48


def normed(values):
    values = values.astype(jnp.float32)
    return values * lax.rsqrt(jnp.mean(values * values, axis=-1, keepdims=True) + 1e-06)


def product(pattern, first_operand, second_operand):
    return jnp.einsum(pattern, first_operand, second_operand, preferred_element_type=jnp.float32)


def split_heads(values):
    return values.reshape(values.shape[:-1] + (HEADS, HEAD))


def merge_heads(values):
    return values.reshape(values.shape[:-2] + (D,))


def usable_keys(first_frame, visible, length):
    frames = jnp.arange(length, dtype=jnp.int32)
    return (frames[None, :] >= first_frame[:, None]) & (
        (visible == 1) | (frames[None, :] == first_frame[:, None])
    )


def time_project(tokens, time_qkv):
    projected = product("ntd,dk->ntk", normed(tokens).astype(jnp.bfloat16), time_qkv)
    time_query = normed(projected[..., :D]).astype(jnp.bfloat16)
    time_key = normed(projected[..., D : 2 * D]).astype(jnp.bfloat16)
    time_value = projected[..., 2 * D :].astype(jnp.bfloat16)
    return (time_query, time_key, time_value)


def time_terms(time_query, key_piece, value_piece, usable):
    scores = product("nqhe,nkhe->nhqk", split_heads(time_query), split_heads(key_piece)) * HEAD ** (
        -0.5
    )
    weights = (jnp.exp(scores) * usable[:, None, None, :].astype(jnp.float32)).astype(jnp.bfloat16)
    numerator = product("nhqk,nkhe->nqhe", weights, split_heads(value_piece))
    denominator = jnp.transpose(jnp.sum(weights.astype(jnp.float32), axis=-1), (0, 2, 1))
    return (numerator, denominator)


def time_finish(tokens, numerator, denominator, time_output, expand, shrink):
    time_mixed = merge_heads(numerator / denominator[..., None]).astype(jnp.bfloat16)
    middle = tokens.astype(jnp.float32) + product("ntd,dk->ntk", time_mixed, time_output)
    middle_norm = normed(middle).astype(jnp.bfloat16)
    hidden = jax.nn.gelu(product("ntd,df->ntf", middle_norm, expand), approximate=True).astype(
        jnp.bfloat16
    )
    return (middle + product("ntf,fd->ntd", hidden, shrink)).astype(jnp.bfloat16)


def track_complete(whole, first_frame, visible, time_qkv, time_output, expand, shrink):
    half_tracks = whole.shape[0]
    core_index = lax.axis_index("frames")
    own_first = lax.dynamic_slice_in_dim(first_frame, core_index * half_tracks, half_tracks, 0)
    own_visible = lax.dynamic_slice_in_dim(visible, core_index * half_tracks, half_tracks, 0)
    time_query, time_key, time_value = time_project(whole, time_qkv)
    usable = usable_keys(own_first, own_visible, whole.shape[1])
    numerator, denominator = time_terms(time_query, time_key, time_value, usable)
    return time_finish(whole, numerator, denominator, time_output, expand, shrink)


def attend_pair(query, key, value, query_form, value_form):
    weights = jnp.exp(
        product(query_form, split_heads(query), split_heads(key)) * HEAD ** (-0.5)
    ).astype(jnp.bfloat16)
    numerator = product(value_form, weights, split_heads(value))
    return (weights, numerator)


def virtual_block(
    settled,
    virtual_init,
    cross_query,
    cross_kv,
    cross_output,
    self_qkv,
    self_output,
    back_query,
    back_kv,
    back_output,
):
    settled_norm = normed(settled).astype(jnp.bfloat16)
    crossed = product("nfd,dk->nfk", settled_norm, cross_kv)
    track_key = normed(crossed[..., :D]).astype(jnp.bfloat16)
    track_value = crossed[..., D:].astype(jnp.bfloat16)
    virtual_norm = normed(virtual_init).astype(jnp.bfloat16)
    virtual_query = normed(product("jd,dk->jk", virtual_norm, cross_query)).astype(jnp.bfloat16)
    cross_weight, numerator = attend_pair(
        virtual_query, track_key, track_value, "jhe,nfhe->fhjn", "fhjn,nfhe->fjhe"
    )
    totals = jnp.transpose(jnp.sum(cross_weight.astype(jnp.float32), axis=-1), (0, 2, 1))
    cross_mixed = merge_heads(numerator / totals[..., None]).astype(jnp.bfloat16)
    virtual_first = virtual_init.astype(jnp.float32)[None] + product(
        "fjd,dk->fjk", cross_mixed, cross_output
    )
    selfed = product("fjd,dk->fjk", normed(virtual_first).astype(jnp.bfloat16), self_qkv)
    self_query = normed(selfed[..., :D]).astype(jnp.bfloat16)
    self_key = normed(selfed[..., D : 2 * D]).astype(jnp.bfloat16)
    self_value = selfed[..., 2 * D :].astype(jnp.bfloat16)
    self_weight, numerator = attend_pair(
        self_query, self_key, self_value, "fjhe,fihe->fhji", "fhji,fihe->fjhe"
    )
    totals = jnp.transpose(jnp.sum(self_weight.astype(jnp.float32), axis=-1), (0, 2, 1))
    self_mixed = merge_heads(numerator / totals[..., None]).astype(jnp.bfloat16)
    virtual_second = virtual_first + product("fjd,dk->fjk", self_mixed, self_output)
    backed = product("fjd,dk->fjk", normed(virtual_second).astype(jnp.bfloat16), back_kv)
    virtual_key = normed(backed[..., :D]).astype(jnp.bfloat16)
    virtual_value = backed[..., D:].astype(jnp.bfloat16)
    track_query = normed(product("nfd,dk->nfk", settled_norm, back_query)).astype(jnp.bfloat16)
    back_weight, numerator = attend_pair(
        track_query, virtual_key, virtual_value, "nfhe,fjhe->nfhj", "nfhj,fjhe->nfhe"
    )
    totals = jnp.sum(back_weight.astype(jnp.float32), axis=-1)
    back_mixed = merge_heads(numerator / totals[..., None]).astype(jnp.bfloat16)
    return (settled.astype(jnp.float32) + product("nfd,dk->nfk", back_mixed, back_output)).astype(
        jnp.bfloat16
    )


def per_device(
    tokens,
    first_frame,
    visible,
    time_qkv,
    time_output,
    expand,
    shrink,
    virtual_init,
    cross_query,
    cross_kv,
    cross_output,
    self_qkv,
    self_output,
    back_query,
    back_kv,
    back_output,
):
    whole = lax.all_to_all(tokens, "frames", split_axis=0, concat_axis=1, tiled=True)
    settled = track_complete(whole, first_frame, visible, time_qkv, time_output, expand, shrink)
    spread = lax.all_to_all(settled, ("tracks", "frames"), split_axis=1, concat_axis=0, tiled=True)
    joined = lax.all_to_all(
        virtual_block(
            spread,
            virtual_init,
            cross_query,
            cross_kv,
            cross_output,
            self_qkv,
            self_output,
            back_query,
            back_kv,
            back_output,
        ),
        ("tracks", "frames"),
        split_axis=0,
        concat_axis=1,
        tiled=True,
    )
    tracked = lax.all_to_all(joined, "frames", split_axis=1, concat_axis=0, tiled=True)
    return tracked


def row_scale(values):
    return lax.rsqrt(jnp.mean(values * values, axis=-1, keepdims=True) + 1e-06)


def unit(values):
    return values * row_scale(values)


def dot(first, second):
    return jnp.dot(first, second, preferred_element_type=jnp.float32)


def dot_t(first, second):
    return lax.dot_general(
        first, second, (((1,), (1,)), ((), ())), preferred_element_type=jnp.float32
    )


WIN = 256
GROUP = HEADS // 2
USED = GROUP * HEAD
SHIFT = D - WIN
STARTS = (0, SHIFT)
BASES = (0, USED - SHIFT)
SPARE = (USED, 0)
LOG2E = 1.4426950408889634
QSCALE = HEAD ** (-0.5) * LOG2E


def head_mask(group, head, rows):
    lane = lax.broadcasted_iota(jnp.int32, (rows, WIN), 1)
    low = BASES[group] + head * HEAD
    return (lane >= low) & (lane < low + HEAD)


def window(values, group):
    return values[:, STARTS[group] : STARTS[group] + WIN]


def with_ones(values, group):
    part = window(values, group)
    lane = lax.broadcasted_iota(jnp.int32, part.shape, 1)
    inside = (lane >= BASES[group]) & (lane < BASES[group] + USED)
    return jnp.where(inside, part, jnp.ones_like(part))


def join_windows(first, second):
    return jnp.concatenate(
        [first[:, :SHIFT], first[:, SHIFT:] + second[:, :SHIFT], second[:, SHIFT:]], axis=1
    )


def picked(summed, group, head):
    share = 1.0 / summed[:, SPARE[group] : SPARE[group] + 1]
    return jnp.where(head_mask(group, head, summed.shape[0]), summed * share, 0.0)


def head_stack(values, group):
    part = window(values, group)
    return jnp.concatenate(
        [
            jnp.where(head_mask(group, h, part.shape[0]), part, jnp.zeros_like(part))
            for h in range(GROUP)
        ],
        axis=0,
    )


def time_keys(key, value, usable):
    held = []
    for group in range(2):
        values = (with_ones(value, group) * usable).astype(jnp.bfloat16)
        held.append((window(key, group), values))
    return held


def time_attend(query, held):
    halves = []
    for group, (keys, values) in enumerate(held):
        queries = window(query, group)
        total = None
        for head in range(GROUP):
            mask = head_mask(group, head, queries.shape[0])
            own = jnp.where(mask, queries, jnp.zeros_like(queries))
            weights = jnp.exp2(dot_t(own, keys)).astype(jnp.bfloat16)
            part = picked(dot(weights, values), group, head)
            total = part if total is None else total + part
        halves.append(total)
    return join_windows(*halves)


def time_queries(x, w_qkv):
    projected = dot(unit(x).astype(jnp.bfloat16), w_qkv[...])
    query = (unit(projected[:, :D]) * QSCALE).astype(jnp.bfloat16)
    key = unit(projected[:, D : 2 * D]).astype(jnp.bfloat16)
    return query, key, projected[:, 2 * D :]


def time_close(x, mixed, w_out, w_expand, w_shrink):
    middle = x + dot(mixed.astype(jnp.bfloat16), w_out[...])
    inner = dot(unit(middle).astype(jnp.bfloat16), w_expand[...])
    half = 0.5 * inner
    bent = jnp.tanh(inner * (0.7978845608028654 + 0.035677408136300125 * (inner * inner)))
    hidden = (half + half * bent).astype(jnp.bfloat16)
    return middle + dot(hidden, w_shrink[...])


def stacked_attention(queries, keys, values, ones_stack):
    nums, dens = [], []
    for group in range(2):
        weights = jnp.exp2(dot_t(window(queries, group), head_stack(keys, group))).astype(
            jnp.bfloat16
        )
        nums.append(dot(weights, head_stack(values, group)))
        dens.append(dot(weights, ones_stack[group]))
    return join_windows(*nums) / join_windows(*dens)


def frame_rows(s, query_stack, ones_stack, virtual, frames, refs):
    w_ckv, w_cout, w_sqkv, w_sout, w_bq, w_bkv, w_bout = refs
    tracks = s.shape[0] // frames
    virt = virtual.shape[0]
    sf = s.astype(jnp.float32)
    sn = unit(sf).astype(jnp.bfloat16)
    crossed = dot(sn, w_ckv[...])
    track_key = unit(crossed[:, :D]).astype(jnp.bfloat16)
    track_value = crossed[:, D:].astype(jnp.bfloat16)
    track_query = (unit(dot(sn, w_bq[...])) * QSCALE).astype(jnp.bfloat16)
    mixed = []
    for i in range(frames):
        rows = slice(i * tracks, (i + 1) * tracks)
        halves = []
        for group in range(2):
            weights = jnp.exp2(
                dot_t(query_stack[group], window(track_key[rows], group))
            ).astype(jnp.bfloat16)
            summed = dot(weights, with_ones(track_value[rows], group))
            total = None
            for head in range(GROUP):
                part = picked(summed[head * virt : (head + 1) * virt], group, head)
                total = part if total is None else total + part
            halves.append(total)
        mixed.append(join_windows(*halves))
    mixed = jnp.concatenate(mixed, axis=0).astype(jnp.bfloat16)
    first = jnp.concatenate([virtual] * frames, axis=0) + dot(mixed, w_cout[...])
    selfed = dot(unit(first).astype(jnp.bfloat16), w_sqkv[...])
    self_query = (unit(selfed[:, :D]) * QSCALE).astype(jnp.bfloat16)
    self_key = unit(selfed[:, D : 2 * D]).astype(jnp.bfloat16)
    self_value = selfed[:, 2 * D :].astype(jnp.bfloat16)
    mixed = []
    for i in range(frames):
        rows = slice(i * virt, (i + 1) * virt)
        mixed.append(
            stacked_attention(self_query[rows], self_key[rows], self_value[rows], ones_stack)
        )
    mixed = jnp.concatenate(mixed, axis=0).astype(jnp.bfloat16)
    second = first + dot(mixed, w_sout[...])
    backed = dot(unit(second).astype(jnp.bfloat16), w_bkv[...])
    virtual_key = unit(backed[:, :D]).astype(jnp.bfloat16)
    virtual_value = backed[:, D:].astype(jnp.bfloat16)
    mixed = []
    for i in range(frames):
        rows = slice(i * tracks, (i + 1) * tracks)
        cols = slice(i * virt, (i + 1) * virt)
        mixed.append(
            stacked_attention(track_query[rows], virtual_key[cols], virtual_value[cols], ones_stack)
        )
    mixed = jnp.concatenate(mixed, axis=0).astype(jnp.bfloat16)
    return (sf + dot(mixed, w_bout[...])).astype(jnp.bfloat16)


STEP_FRAMES = 4
SINGLE_TRACKS = 2
SHARED = SINGLE_TRACKS - 1
STEP_TRACKS = 2
EARLY_PAIRS = 0
OCTET = 8
VMEM_BYTES = 62 * 1024 * 1024
MESH = pl.DeviceIdType.MESH
OUT = pltpu.VMEM


def turn_matrix(side, mine, cores, own_frames):
    pairs = (mine - SINGLE_TRACKS) // STEP_TRACKS
    single_rows = cores * SINGLE_TRACKS * own_frames
    pair_rows = cores * pairs * STEP_TRACKS * OCTET
    tracks = cores * mine
    shape = (OCTET * tracks, single_rows + pair_rows)
    row = lax.broadcasted_iota(jnp.int32, shape, 0)
    col = lax.broadcasted_iota(jnp.int32, shape, 1)
    frame, track = row // tracks, row % tracks
    core, n = track // mine, track % mine
    single = (core * SINGLE_TRACKS + n) * own_frames + side * OCTET + frame
    late = n - SINGLE_TRACKS
    pair = single_rows + (core * pairs + late // STEP_TRACKS) * (STEP_TRACKS * OCTET)
    pair = pair + (late % STEP_TRACKS) * OCTET + frame
    source = jnp.where(late < 0, single, pair)
    return jnp.where(col == source, 1.0, 0.0).astype(jnp.bfloat16)


def partner(me, count, k):
    half = count // 2
    inner = lax.rem((me * 4 // count + 1) // 2, 2)
    step = inner * k + (1 - inner) * (count - 2 - k)
    turn = step // half
    side = lax.rem(me // half + 1 + turn, 2)
    return side * half + lax.rem(lax.rem(me, half) + lax.rem(step, half) + turn, half)


def ordered(me, count, k):
    half = count // 2
    side = me // half
    cross = (1 - side) * half + k
    near = side * half + (k - half) + jnp.where(side * half + (k - half) >= me, 1, 0)
    return jnp.where(k < half, cross, near)


def layer_kernel(n_tracks_axis, n_frames_axis, n_weights, *refs):
    tokens, first_frame, visible, virtual_init = refs[:4]
    stored = refs[4 : 4 + n_weights]
    returned = refs[4 + n_weights]
    loaded = refs[5 + n_weights : 5 + 2 * n_weights]
    (
        own,
        other,
        settled_one,
        settled_two,
        settled_near,
        raw,
        mate_rows,
        mate_usable,
        flag_rows,
        spread_one,
        spread_two,
        by_frame,
        result,
        query_stack,
        ones_stack,
        usable,
        swap,
        weight_sem,
        own_sem,
        pair_send,
        pair_recv,
        spread_send,
        spread_recv,
        back_send,
        back_recv,
        raw_send,
        raw_recv,
    ) = refs[5 + 2 * n_weights :]
    w_qkv, w_out, w_expand, w_shrink, w_cq = loaded[:5]
    late = loaded[5:]
    t = lax.axis_index("tracks")
    f = lax.axis_index("frames")
    group_index = lax.axis_index("groups")
    devices = n_tracks_axis * n_frames_axis
    me = t * n_frames_axis + f
    held, part, _ = tokens.shape
    mine = held // n_frames_axis
    length = part * n_frames_axis
    own_frames = length // devices
    all_tracks = held * n_tracks_axis
    virt = virtual_init.shape[0]
    pairs = (mine - SINGLE_TRACKS) // STEP_TRACKS
    late_pairs = pairs - EARLY_PAIRS
    blocks = own_frames // OCTET
    quarter = n_tracks_axis // 4
    half_devices = devices // 2
    zone = t // quarter
    is_inner = (zone + 1) // 2 % 2
    inner = is_inner == 1
    side_index = t // (n_tracks_axis // 2)
    mate_t = t + (1 - 2 * side_index) * quarter
    mate = mate_t * n_frames_axis + f

    def place(index):
        return (group_index, index // n_frames_axis, index % n_frames_axis)

    barrier = pltpu.get_barrier_semaphore()

    @pl.loop(1, devices, unroll=True)
    def _(k):
        pl.semaphore_signal(
            barrier,
            inc=1,
            device_id=place(lax.rem(me + k, devices)),
            device_id_type=MESH,
        )

    def own_copy(n):
        return pltpu.make_async_copy(tokens.at[f * mine + n], own.at[n], own_sem.at[n])

    loads = [
        pltpu.make_async_copy(stored[k], loaded[k], weight_sem.at[k]) for k in range(n_weights)
    ]
    own_copy(0).start()
    for load in loads[:4]:
        load.start()

    @pl.loop(1, mine)
    def _(n):
        own_copy(n).start()

    for load in loads[4:]:
        load.start()

    ids = lax.broadcasted_iota(jnp.int32, (1, length), 1)
    for n in range(held):
        started = first_frame[n]
        kept = (ids >= started) & ((visible[n : n + 1, :] == 1) | (ids == started))
        flag_rows[n : n + 1, :] = jnp.where(kept, 1.0, 0.0)
    usable[...] = jnp.transpose(flag_rows[...], (1, 0))
    for side in range(blocks):
        swap[side] = turn_matrix(side, mine, n_frames_axis, own_frames)
    for group in range(2):
        ones_stack[group] = jnp.concatenate(
            [
                jnp.where(head_mask(group, h, virt), 1.0, 0.0).astype(jnp.bfloat16)
                for h in range(GROUP)
            ],
            axis=0,
        )

    pl.semaphore_wait(barrier, devices - 1)

    def pair_copy(n):
        return pltpu.make_async_remote_copy(
            src_ref=tokens.at[(1 - f) * mine + n],
            dst_ref=other.at[n],
            send_sem=pair_send.at[n],
            recv_sem=pair_recv.at[n],
            device_id=(group_index, t, 1 - f),
            device_id_type=MESH,
        )

    def raw_copy(core):
        return pltpu.make_async_remote_copy(
            src_ref=tokens.at[core * mine + SHARED],
            dst_ref=raw.at[lax.rem(f + core, n_frames_axis)],
            send_sem=raw_send.at[0],
            recv_sem=raw_recv.at[0],
            device_id=(group_index, mate_t, core),
            device_id_type=MESH,
        )

    pair_copy(0).start()

    @pl.when(inner)
    def _():
        pltpu.make_async_remote_copy(
            src_ref=flag_rows,
            dst_ref=mate_rows,
            send_sem=raw_send.at[1],
            recv_sem=raw_recv.at[1],
            device_id=(group_index, mate_t, f),
            device_id_type=MESH,
        ).start()
        for core in range(n_frames_axis):
            raw_copy(core).start()

    @pl.loop(1, mine)
    def _(n):
        pair_copy(n).start()

    def send(src, dst, sem, index):
        pltpu.make_async_remote_copy(
            src_ref=src,
            dst_ref=dst,
            send_sem=spread_send,
            recv_sem=spread_recv.at[sem],
            device_id=place(index),
            device_id_type=MESH,
        ).start()

    def base_of(index):
        return lax.rem(index + f, n_frames_axis) * part + (index // n_frames_axis) * own_frames

    def send_single(n, side):
        dst = spread_one.at[me, n]

        def source(index):
            at = pl.multiple_of(base_of(index), own_frames)
            return settled_one.at[n, pl.ds(at, own_frames), :]

        core = lax.rem(f + side, n_frames_axis)

        @pl.loop(0, n_tracks_axis - 1, unroll=True)
        def _(k):
            index = ordered(t, n_tracks_axis, k) * n_frames_axis + core
            send(source(index), dst, 0, index)

        if side == 0:
            pltpu.make_async_copy(source(me), dst, spread_recv.at[0]).start()
        else:
            index = t * n_frames_axis + core
            send(source(index), dst, 0, index)

    def send_pairs(p, count, block, n_blocks, sem):
        if n_blocks == blocks:
            dst = spread_two.at[me, p]
        else:
            dst = spread_two.at[me, pl.ds(p, count), block]

        def source(index):
            at = base_of(index) // OCTET + block
            if n_blocks == blocks:
                return settled_two.at[p, pl.ds(at, blocks)]
            return settled_two.at[pl.ds(p, count), at]

        @pl.loop(0, devices - 1, unroll=True)
        def _(k):
            index = ordered(me, devices, k)
            send(source(index), dst, sem, index)

        pltpu.make_async_copy(source(me), dst, spread_recv.at[sem]).start()

    lane = lax.broadcasted_iota(jnp.int32, (part, held), 1)

    def flags_of(table, n):
        chosen = lane == f * mine + n
        column = []
        for side in range(n_frames_axis):
            at = pl.multiple_of(lax.rem(f + side, n_frames_axis) * part, part)
            seen = jnp.where(chosen, table[pl.ds(at, part), :], 0.0)
            column.append(jnp.sum(seen, axis=1, keepdims=True))
        return jnp.concatenate(column, axis=0)

    def gather(n):
        own_copy(n).wait()
        pair_copy(n).wait_recv()
        return [own[n], other[n]], flags_of(usable, n)

    for load in loads[:4]:
        load.wait()

    @pl.loop(0, SINGLE_TRACKS - is_inner)
    def _(n):
        pieces, flags = gather(n)
        x = jnp.concatenate(pieces, axis=0).astype(jnp.float32)
        query, key, value = time_queries(x, w_qkv)
        mixed = time_attend(query, time_keys(key, value, flags))
        done = time_close(x, mixed, w_out, w_expand, w_shrink)
        settled_one[n] = done.astype(jnp.bfloat16)
        for side in range(n_frames_axis):
            send_single(n, side)

    span = part // 2

    def near(values):
        kept = []
        for core in range(n_frames_axis):
            low = values[core * part : core * part + span]
            high = values[core * part + span : (core + 1) * part]
            kept.append(jnp.where(side_index == 0, low, high))
        return jnp.concatenate(kept, axis=0)

    def near_source(k, index):
        at = lax.rem(index + f, n_frames_axis) * span
        at += (index // n_frames_axis - side_index * (n_tracks_axis // 2)) * own_frames
        return settled_near.at[k, pl.ds(pl.multiple_of(at, own_frames), own_frames), :]

    @pl.loop(0, pairs)
    def _(p):
        pieces, flags = [], []
        for k in range(STEP_TRACKS):
            piece, flag = gather(SINGLE_TRACKS + p * STEP_TRACKS + k)
            pieces += piece
            flags.append(flag)
        x = jnp.concatenate(pieces, axis=0).astype(jnp.float32)
        query, key, value = time_queries(x, w_qkv)
        mixed = []
        for k in range(STEP_TRACKS):
            rows = slice(k * length, (k + 1) * length)
            mixed.append(time_attend(query[rows], time_keys(key[rows], value[rows], flags[k])))
        done = time_close(x, jnp.concatenate(mixed, axis=0), w_out, w_expand, w_shrink)
        done = done.reshape(STEP_TRACKS, length // OCTET, OCTET, D)
        done = jnp.transpose(done, (1, 0, 2, 3)).reshape(length // OCTET, STEP_TRACKS * OCTET, D)
        settled_two[p] = done.astype(jnp.bfloat16)

        if EARLY_PAIRS:

            @pl.when(p < EARLY_PAIRS)
            def _():
                send_pairs(p, 1, 0, blocks, 1)

        @pl.when(p >= EARLY_PAIRS)
        def _():
            send_pairs(p, 1, 0, 1, 2)

    for block in range(1, blocks):
        send_pairs(EARLY_PAIRS, late_pairs, block, 1, 2 + block)

    @pl.when(inner)
    def _():
        pieces, flags = gather(SHARED)
        pltpu.make_async_copy(raw, raw, raw_recv.at[0]).wait()
        pltpu.make_async_copy(mate_rows, mate_rows, raw_recv.at[1]).wait()
        mate_usable[...] = jnp.transpose(mate_rows[...], (1, 0))
        flags = [flags, flags_of(mate_usable, SHARED)]
        pieces += [raw[core] for core in range(n_frames_axis)]
        x = jnp.concatenate(pieces, axis=0).astype(jnp.float32)
        query, key, value = time_queries(x, w_qkv)
        mixed, kept = [], []
        for k in range(2):
            rows = slice(k * length, (k + 1) * length)
            keys = time_keys(key[rows], value[rows], flags[k])
            mixed.append(time_attend(near(query[rows]), keys))
            kept.append(near(x[rows]))
        mixed, kept = jnp.concatenate(mixed, axis=0), jnp.concatenate(kept, axis=0)
        done = time_close(kept, mixed, w_out, w_expand, w_shrink)
        settled_near[...] = done.astype(jnp.bfloat16).reshape(2, n_frames_axis * span, D)
        start = side_index * half_devices
        for k, owner in enumerate((me, mate)):
            dst = spread_one.at[owner, SHARED]

            @pl.loop(1, half_devices, unroll=True)
            def _(j):
                index = start + lax.rem(me - start + j, half_devices)
                send(near_source(k, index), dst, 0, index)

            pltpu.make_async_copy(near_source(k, me), dst, spread_recv.at[0]).start()

    for load in loads[4:]:
        load.wait()
    virtual = virtual_init[...].astype(jnp.float32)
    virtual_query = unit(dot(unit(virtual).astype(jnp.bfloat16), w_cq[...])) * QSCALE
    for group in range(2):
        query_stack[group] = head_stack(virtual_query, group).astype(jnp.bfloat16)

    @pl.loop(0, mine)
    def _(n):
        pair_copy(n).wait_send()

    def arrived(ref, sem):
        pltpu.make_async_copy(ref, ref, spread_recv.at[sem]).wait()

    arrived(spread_one, 0)
    if EARLY_PAIRS:
        arrived(spread_two.at[:, pl.ds(0, EARLY_PAIRS)], 1)

    @pl.loop(0, blocks)
    def _(side):
        arrived(spread_two.at[:, pl.ds(EARLY_PAIRS, late_pairs), 0], 2 + side)
        at_frame = pl.multiple_of(side * OCTET, OCTET)

        @pl.loop(0, n_tracks_axis)
        def _(c):
            one = spread_one[pl.ds(c * n_frames_axis, n_frames_axis)]
            two = spread_two[pl.ds(c * n_frames_axis, n_frames_axis), :, side]
            rows = jnp.concatenate([one.reshape(-1, D), two.reshape(-1, D)], axis=0)
            turned = dot(swap[side], rows).astype(jnp.bfloat16)
            at = pl.multiple_of(c * held, held)
            by_frame[pl.ds(at_frame, OCTET), pl.ds(at, held), :] = turned.reshape(OCTET, held, D)

        @pl.loop(0, OCTET // STEP_FRAMES)
        def _(step):
            f0 = side * OCTET + step * STEP_FRAMES
            s = by_frame[pl.ds(f0, STEP_FRAMES)].reshape(STEP_FRAMES * all_tracks, D)
            done = frame_rows(
                s,
                query_stack,
                ones_stack,
                virtual_init[...].astype(jnp.float32),
                STEP_FRAMES,
                late,
            )
            result[pl.ds(f0, STEP_FRAMES)] = done.reshape(STEP_FRAMES, all_tracks, D)
            dst = returned.at[t, pl.ds(f0, STEP_FRAMES)]

            def source(index):
                return result.at[
                    pl.ds(f0, STEP_FRAMES), pl.ds(pl.multiple_of(index * held, held), held), :
                ]

            @pl.loop(0, n_tracks_axis - 1, unroll=True)
            def _(k):
                index = ordered(t, n_tracks_axis, k)
                pltpu.make_async_remote_copy(
                    src_ref=source(index),
                    dst_ref=dst,
                    send_sem=back_send,
                    recv_sem=back_recv,
                    device_id=(group_index, index, f),
                    device_id_type=MESH,
                ).start()

            pltpu.make_async_copy(source(t), dst, back_recv).start()

    others = length - own_frames
    sent = settled_one.at[pl.ds(0, SHARED), pl.ds(0, others), :]
    pltpu.make_async_copy(sent, sent, spread_send).wait()

    @pl.when(inner)
    def _():
        sent = settled_near.at[:, pl.ds(0, part - own_frames), :]
        pltpu.make_async_copy(sent, sent, spread_send).wait()
        pltpu.make_async_copy(raw, raw, raw_send.at[0]).wait()
        pltpu.make_async_copy(mate_rows, mate_rows, raw_send.at[1]).wait()

    @pl.when(is_inner == 0)
    def _():
        sent = settled_one.at[SHARED, pl.ds(0, others), :]
        pltpu.make_async_copy(sent, sent, spread_send).wait()

    sent = settled_two.at[:, pl.ds(0, others // OCTET)]
    pltpu.make_async_copy(sent, sent, spread_send).wait()
    sent = result.at[:, pl.ds(0, all_tracks - held), :]
    pltpu.make_async_copy(sent, sent, back_send).wait()
    pltpu.make_async_copy(returned, returned, back_recv).wait()


def fused_device(n_tracks_axis, n_frames_axis, tokens, first_frame, visible, *rest):
    (w_qkv, w_out, w_expand, w_shrink, virtual_init, w_cq, *late) = rest
    weights = (w_qkv, w_out, w_expand, w_shrink, w_cq, *late)
    held, part, _ = tokens.shape
    mine = held // n_frames_axis
    length = part * n_frames_axis
    devices = n_tracks_axis * n_frames_axis
    own_frames = length // devices
    all_tracks = held * n_tracks_axis
    pairs = (mine - SINGLE_TRACKS) // STEP_TRACKS
    unit_rows = STEP_TRACKS * OCTET
    blocks = own_frames // OCTET
    vmem = pl.BlockSpec(memory_space=pltpu.VMEM)
    hbm = pl.BlockSpec(memory_space=pltpu.HBM)
    virt = virtual_init.shape[0]
    bf16 = jnp.bfloat16
    dma = pltpu.SemaphoreType.DMA
    turn_rows = n_frames_axis * (SINGLE_TRACKS * own_frames + pairs * unit_rows)
    returned = pl.pallas_call(
        functools.partial(layer_kernel, n_tracks_axis, n_frames_axis, len(weights)),
        out_shape=OUT((n_tracks_axis, own_frames, held, D), bf16),
        in_specs=[hbm, pl.BlockSpec(memory_space=pltpu.SMEM), vmem, vmem] + [hbm] * len(weights),
        out_specs=pl.BlockSpec(memory_space=OUT),
        scratch_shapes=[pltpu.VMEM(w.shape, w.dtype) for w in weights]
        + [
            pltpu.VMEM((mine, part, D), bf16),
            pltpu.VMEM((mine, part, D), bf16),
            pltpu.VMEM((SINGLE_TRACKS, length, D), bf16),
            pltpu.VMEM((pairs, length // OCTET, unit_rows, D), bf16),
            pltpu.VMEM((2, part, D), bf16),
            pltpu.VMEM((n_frames_axis, part, D), bf16),
            pltpu.VMEM((held, length), jnp.float32),
            pltpu.VMEM((length, held), jnp.float32),
            pltpu.VMEM((held, length), jnp.float32),
            pltpu.VMEM((devices, SINGLE_TRACKS, own_frames, D), bf16),
            pltpu.VMEM((devices, pairs, blocks, unit_rows, D), bf16),
            pltpu.VMEM((own_frames, all_tracks, D), bf16),
            pltpu.VMEM((own_frames, all_tracks, D), bf16),
            pltpu.VMEM((2, GROUP * virt, WIN), bf16),
            pltpu.VMEM((2, GROUP * virt, WIN), bf16),
            pltpu.VMEM((length, held), jnp.float32),
            pltpu.VMEM((blocks, OCTET * held, turn_rows), bf16),
            dma((len(weights),)),
            dma((mine,)),
            dma((mine,)),
            dma((mine,)),
            dma,
            dma((2 + blocks,)),
            dma,
            dma,
            dma((2,)),
            dma((2,)),
        ],
        compiler_params=pltpu.CompilerParams(
            collective_id=0, has_side_effects=True, vmem_limit_bytes=VMEM_BYTES
        ),
    )(tokens, first_frame, visible, virtual_init, *weights)
    return jnp.transpose(returned, (2, 0, 1, 3)).reshape(tokens.shape)


def fits(tracks_axis, frames_axis, tokens):
    held = tokens.shape[0]
    own_frames = tokens.shape[1] // tracks_axis
    mine = held // 2
    return (
        frames_axis == 2
        and tracks_axis % 4 == 0
        and mine > SINGLE_TRACKS
        and (mine - SINGLE_TRACKS) % STEP_TRACKS == 0
        and own_frames == held
        and own_frames == 2 * OCTET
        and STEP_TRACKS * OCTET == 16
        and tokens.shape[1] % 128 == 0
    )


def solution(mesh):
    placed = (
        P(("groups", "tracks"), "frames", None),
        P(("groups", "tracks")),
        P(("groups", "tracks"), None),
        P(),
        P(),
        P(),
        P(),
        P(),
        P(),
        P(),
        P(),
        P(),
        P(),
        P(),
        P(),
        P(),
    )
    axes = (mesh.shape["tracks"], mesh.shape["frames"])

    def body(tokens, *rest):
        if fits(*axes, tokens):
            return fused_device(*axes, tokens, *rest)
        return per_device(tokens, *rest)

    return jax.shard_map(
        body,
        mesh=mesh,
        in_specs=placed,
        out_specs=P(("groups", "tracks"), "frames", None),
        check_vma=False,
    )
```

```python
import functools

import jax
import jax.numpy as jnp
from jax import lax
from jax.experimental import pallas as pl
from jax.experimental.pallas import tpu as pltpu
from jax.sharding import PartitionSpec as P

D = 384
HEADS = 8
HEAD = 48


def normed(values):
    values = values.astype(jnp.float32)
    return values * lax.rsqrt(jnp.mean(values * values, axis=-1, keepdims=True) + 1e-06)


def product(pattern, first_operand, second_operand):
    return jnp.einsum(pattern, first_operand, second_operand, preferred_element_type=jnp.float32)


def split_heads(values):
    return values.reshape(values.shape[:-1] + (HEADS, HEAD))


def merge_heads(values):
    return values.reshape(values.shape[:-2] + (D,))


def usable_keys(first_frame, visible, length):
    frames = jnp.arange(length, dtype=jnp.int32)
    return (frames[None, :] >= first_frame[:, None]) & (
        (visible == 1) | (frames[None, :] == first_frame[:, None])
    )


def time_project(tokens, time_qkv):
    projected = product("ntd,dk->ntk", normed(tokens).astype(jnp.bfloat16), time_qkv)
    time_query = normed(projected[..., :D]).astype(jnp.bfloat16)
    time_key = normed(projected[..., D : 2 * D]).astype(jnp.bfloat16)
    time_value = projected[..., 2 * D :].astype(jnp.bfloat16)
    return (time_query, time_key, time_value)


def time_terms(time_query, key_piece, value_piece, usable):
    scores = product("nqhe,nkhe->nhqk", split_heads(time_query), split_heads(key_piece)) * HEAD ** (
        -0.5
    )
    weights = (jnp.exp(scores) * usable[:, None, None, :].astype(jnp.float32)).astype(jnp.bfloat16)
    numerator = product("nhqk,nkhe->nqhe", weights, split_heads(value_piece))
    denominator = jnp.transpose(jnp.sum(weights.astype(jnp.float32), axis=-1), (0, 2, 1))
    return (numerator, denominator)


def time_finish(tokens, numerator, denominator, time_output, expand, shrink):
    time_mixed = merge_heads(numerator / denominator[..., None]).astype(jnp.bfloat16)
    middle = tokens.astype(jnp.float32) + product("ntd,dk->ntk", time_mixed, time_output)
    middle_norm = normed(middle).astype(jnp.bfloat16)
    hidden = jax.nn.gelu(product("ntd,df->ntf", middle_norm, expand), approximate=True).astype(
        jnp.bfloat16
    )
    return (middle + product("ntf,fd->ntd", hidden, shrink)).astype(jnp.bfloat16)


def track_complete(whole, first_frame, visible, time_qkv, time_output, expand, shrink):
    half_tracks = whole.shape[0]
    core_index = lax.axis_index("frames")
    own_first = lax.dynamic_slice_in_dim(first_frame, core_index * half_tracks, half_tracks, 0)
    own_visible = lax.dynamic_slice_in_dim(visible, core_index * half_tracks, half_tracks, 0)
    time_query, time_key, time_value = time_project(whole, time_qkv)
    usable = usable_keys(own_first, own_visible, whole.shape[1])
    numerator, denominator = time_terms(time_query, time_key, time_value, usable)
    return time_finish(whole, numerator, denominator, time_output, expand, shrink)


def attend_pair(query, key, value, query_form, value_form):
    weights = jnp.exp(
        product(query_form, split_heads(query), split_heads(key)) * HEAD ** (-0.5)
    ).astype(jnp.bfloat16)
    numerator = product(value_form, weights, split_heads(value))
    return (weights, numerator)


def virtual_block(
    settled,
    virtual_init,
    cross_query,
    cross_kv,
    cross_output,
    self_qkv,
    self_output,
    back_query,
    back_kv,
    back_output,
):
    settled_norm = normed(settled).astype(jnp.bfloat16)
    crossed = product("nfd,dk->nfk", settled_norm, cross_kv)
    track_key = normed(crossed[..., :D]).astype(jnp.bfloat16)
    track_value = crossed[..., D:].astype(jnp.bfloat16)
    virtual_norm = normed(virtual_init).astype(jnp.bfloat16)
    virtual_query = normed(product("jd,dk->jk", virtual_norm, cross_query)).astype(jnp.bfloat16)
    cross_weight, numerator = attend_pair(
        virtual_query, track_key, track_value, "jhe,nfhe->fhjn", "fhjn,nfhe->fjhe"
    )
    totals = jnp.transpose(jnp.sum(cross_weight.astype(jnp.float32), axis=-1), (0, 2, 1))
    cross_mixed = merge_heads(numerator / totals[..., None]).astype(jnp.bfloat16)
    virtual_first = virtual_init.astype(jnp.float32)[None] + product(
        "fjd,dk->fjk", cross_mixed, cross_output
    )
    selfed = product("fjd,dk->fjk", normed(virtual_first).astype(jnp.bfloat16), self_qkv)
    self_query = normed(selfed[..., :D]).astype(jnp.bfloat16)
    self_key = normed(selfed[..., D : 2 * D]).astype(jnp.bfloat16)
    self_value = selfed[..., 2 * D :].astype(jnp.bfloat16)
    self_weight, numerator = attend_pair(
        self_query, self_key, self_value, "fjhe,fihe->fhji", "fhji,fihe->fjhe"
    )
    totals = jnp.transpose(jnp.sum(self_weight.astype(jnp.float32), axis=-1), (0, 2, 1))
    self_mixed = merge_heads(numerator / totals[..., None]).astype(jnp.bfloat16)
    virtual_second = virtual_first + product("fjd,dk->fjk", self_mixed, self_output)
    backed = product("fjd,dk->fjk", normed(virtual_second).astype(jnp.bfloat16), back_kv)
    virtual_key = normed(backed[..., :D]).astype(jnp.bfloat16)
    virtual_value = backed[..., D:].astype(jnp.bfloat16)
    track_query = normed(product("nfd,dk->nfk", settled_norm, back_query)).astype(jnp.bfloat16)
    back_weight, numerator = attend_pair(
        track_query, virtual_key, virtual_value, "nfhe,fjhe->nfhj", "nfhj,fjhe->nfhe"
    )
    totals = jnp.sum(back_weight.astype(jnp.float32), axis=-1)
    back_mixed = merge_heads(numerator / totals[..., None]).astype(jnp.bfloat16)
    return (settled.astype(jnp.float32) + product("nfd,dk->nfk", back_mixed, back_output)).astype(
        jnp.bfloat16
    )


def per_device(
    tokens,
    first_frame,
    visible,
    time_qkv,
    time_output,
    expand,
    shrink,
    virtual_init,
    cross_query,
    cross_kv,
    cross_output,
    self_qkv,
    self_output,
    back_query,
    back_kv,
    back_output,
):
    whole = lax.all_to_all(tokens, "frames", split_axis=0, concat_axis=1, tiled=True)
    settled = track_complete(whole, first_frame, visible, time_qkv, time_output, expand, shrink)
    spread = lax.all_to_all(settled, ("tracks", "frames"), split_axis=1, concat_axis=0, tiled=True)
    joined = lax.all_to_all(
        virtual_block(
            spread,
            virtual_init,
            cross_query,
            cross_kv,
            cross_output,
            self_qkv,
            self_output,
            back_query,
            back_kv,
            back_output,
        ),
        ("tracks", "frames"),
        split_axis=0,
        concat_axis=1,
        tiled=True,
    )
    tracked = lax.all_to_all(joined, "frames", split_axis=1, concat_axis=0, tiled=True)
    return tracked


def row_scale(values):
    return lax.rsqrt(jnp.mean(values * values, axis=-1, keepdims=True) + 1e-06)


def unit(values):
    return values * row_scale(values)


def dot(first, second):
    return jnp.dot(first, second, preferred_element_type=jnp.float32)


def dot_t(first, second):
    return lax.dot_general(
        first, second, (((1,), (1,)), ((), ())), preferred_element_type=jnp.float32
    )


WIN = 256
GROUP = HEADS // 2
USED = GROUP * HEAD
SHIFT = D - WIN
STARTS = (0, SHIFT)
BASES = (0, USED - SHIFT)
SPARE = (USED, 0)
LOG2E = 1.4426950408889634
QSCALE = HEAD ** (-0.5) * LOG2E


def head_mask(group, head, rows):
    lane = lax.broadcasted_iota(jnp.int32, (rows, WIN), 1)
    low = BASES[group] + head * HEAD
    return (lane >= low) & (lane < low + HEAD)


def window(values, group):
    return values[:, STARTS[group] : STARTS[group] + WIN]


def with_ones(values, group):
    part = window(values, group)
    lane = lax.broadcasted_iota(jnp.int32, part.shape, 1)
    inside = (lane >= BASES[group]) & (lane < BASES[group] + USED)
    return jnp.where(inside, part, jnp.ones_like(part))


def join_windows(first, second):
    return jnp.concatenate(
        [first[:, :SHIFT], first[:, SHIFT:] + second[:, :SHIFT], second[:, SHIFT:]], axis=1
    )


def picked(summed, group, head):
    share = 1.0 / summed[:, SPARE[group] : SPARE[group] + 1]
    return jnp.where(head_mask(group, head, summed.shape[0]), summed * share, 0.0)


def head_stack(values, group):
    part = window(values, group)
    return jnp.concatenate(
        [
            jnp.where(head_mask(group, h, part.shape[0]), part, jnp.zeros_like(part))
            for h in range(GROUP)
        ],
        axis=0,
    )


def time_keys(key, value, usable):
    held = []
    for group in range(2):
        values = (with_ones(value, group) * usable).astype(jnp.bfloat16)
        held.append((window(key, group), values))
    return held


def time_attend(query, held):
    halves = []
    for group, (keys, values) in enumerate(held):
        queries = window(query, group)
        total = None
        for head in range(GROUP):
            mask = head_mask(group, head, queries.shape[0])
            own = jnp.where(mask, queries, jnp.zeros_like(queries))
            weights = jnp.exp2(dot_t(own, keys)).astype(jnp.bfloat16)
            part = picked(dot(weights, values), group, head)
            total = part if total is None else total + part
        halves.append(total)
    return join_windows(*halves)


def time_queries(x, w_qkv):
    projected = dot(unit(x).astype(jnp.bfloat16), w_qkv[...])
    query = (unit(projected[:, :D]) * QSCALE).astype(jnp.bfloat16)
    key = unit(projected[:, D : 2 * D]).astype(jnp.bfloat16)
    return query, key, projected[:, 2 * D :]


def time_close(x, mixed, w_out, w_expand, w_shrink):
    middle = x + dot(mixed.astype(jnp.bfloat16), w_out[...])
    inner = dot(unit(middle).astype(jnp.bfloat16), w_expand[...])
    half = 0.5 * inner
    bent = jnp.tanh(inner * (0.7978845608028654 + 0.035677408136300125 * (inner * inner)))
    hidden = (half + half * bent).astype(jnp.bfloat16)
    return middle + dot(hidden, w_shrink[...])


def stacked_attention(queries, keys, values, ones_stack):
    nums, dens = [], []
    for group in range(2):
        weights = jnp.exp2(dot_t(window(queries, group), head_stack(keys, group))).astype(
            jnp.bfloat16
        )
        nums.append(dot(weights, head_stack(values, group)))
        dens.append(dot(weights, ones_stack[group]))
    return join_windows(*nums) / join_windows(*dens)


def frame_rows(s, query_stack, ones_stack, virtual, frames, refs):
    w_ckv, w_cout, w_sqkv, w_sout, w_bq, w_bkv, w_bout = refs
    tracks = s.shape[0] // frames
    virt = virtual.shape[0]
    sf = s.astype(jnp.float32)
    sn = unit(sf).astype(jnp.bfloat16)
    crossed = dot(sn, w_ckv[...])
    track_key = unit(crossed[:, :D]).astype(jnp.bfloat16)
    track_value = crossed[:, D:].astype(jnp.bfloat16)
    track_query = (unit(dot(sn, w_bq[...])) * QSCALE).astype(jnp.bfloat16)
    mixed = []
    for i in range(frames):
        rows = slice(i * tracks, (i + 1) * tracks)
        halves = []
        for group in range(2):
            weights = jnp.exp2(
                dot_t(query_stack[group], window(track_key[rows], group))
            ).astype(jnp.bfloat16)
            summed = dot(weights, with_ones(track_value[rows], group))
            total = None
            for head in range(GROUP):
                part = picked(summed[head * virt : (head + 1) * virt], group, head)
                total = part if total is None else total + part
            halves.append(total)
        mixed.append(join_windows(*halves))
    mixed = jnp.concatenate(mixed, axis=0).astype(jnp.bfloat16)
    first = jnp.concatenate([virtual] * frames, axis=0) + dot(mixed, w_cout[...])
    selfed = dot(unit(first).astype(jnp.bfloat16), w_sqkv[...])
    self_query = (unit(selfed[:, :D]) * QSCALE).astype(jnp.bfloat16)
    self_key = unit(selfed[:, D : 2 * D]).astype(jnp.bfloat16)
    self_value = selfed[:, 2 * D :].astype(jnp.bfloat16)
    mixed = []
    for i in range(frames):
        rows = slice(i * virt, (i + 1) * virt)
        mixed.append(
            stacked_attention(self_query[rows], self_key[rows], self_value[rows], ones_stack)
        )
    mixed = jnp.concatenate(mixed, axis=0).astype(jnp.bfloat16)
    second = first + dot(mixed, w_sout[...])
    backed = dot(unit(second).astype(jnp.bfloat16), w_bkv[...])
    virtual_key = unit(backed[:, :D]).astype(jnp.bfloat16)
    virtual_value = backed[:, D:].astype(jnp.bfloat16)
    mixed = []
    for i in range(frames):
        rows = slice(i * tracks, (i + 1) * tracks)
        cols = slice(i * virt, (i + 1) * virt)
        mixed.append(
            stacked_attention(track_query[rows], virtual_key[cols], virtual_value[cols], ones_stack)
        )
    mixed = jnp.concatenate(mixed, axis=0).astype(jnp.bfloat16)
    return (sf + dot(mixed, w_bout[...])).astype(jnp.bfloat16)


STEP_FRAMES = 4
SINGLE_TRACKS = 2
SHARED = SINGLE_TRACKS - 1
STEP_TRACKS = 2
EARLY_PAIRS = 0
OCTET = 8
VMEM_BYTES = 62 * 1024 * 1024
MESH = pl.DeviceIdType.MESH
OUT = pltpu.VMEM


def turn_matrix(side, mine, cores, own_frames):
    pairs = (mine - SINGLE_TRACKS) // STEP_TRACKS
    single_rows = cores * SINGLE_TRACKS * own_frames
    pair_rows = cores * pairs * STEP_TRACKS * OCTET
    tracks = cores * mine
    shape = (OCTET * tracks, single_rows + pair_rows)
    row = lax.broadcasted_iota(jnp.int32, shape, 0)
    col = lax.broadcasted_iota(jnp.int32, shape, 1)
    frame, track = row // tracks, row % tracks
    core, n = track // mine, track % mine
    single = (core * SINGLE_TRACKS + n) * own_frames + side * OCTET + frame
    late = n - SINGLE_TRACKS
    pair = single_rows + (core * pairs + late // STEP_TRACKS) * (STEP_TRACKS * OCTET)
    pair = pair + (late % STEP_TRACKS) * OCTET + frame
    source = jnp.where(late < 0, single, pair)
    return jnp.where(col == source, 1.0, 0.0).astype(jnp.bfloat16)


def partner(me, count, k):
    half = count // 2
    inner = lax.rem((me * 4 // count + 1) // 2, 2)
    step = inner * k + (1 - inner) * (count - 2 - k)
    turn = step // half
    side = lax.rem(me // half + 1 + turn, 2)
    return side * half + lax.rem(lax.rem(me, half) + lax.rem(step, half) + turn, half)


def ordered(me, count, k):
    half = count // 2
    side = me // half
    cross = (1 - side) * half + k
    near = side * half + (k - half) + jnp.where(side * half + (k - half) >= me, 1, 0)
    return jnp.where(k < half, cross, near)


def layer_kernel(n_tracks_axis, n_frames_axis, n_weights, *refs):
    tokens, first_frame_in, visible_in, virtual_in = refs[:4]
    stored = refs[4 : 4 + n_weights]
    returned = refs[4 + n_weights]
    loaded = refs[5 + n_weights : 5 + 2 * n_weights]
    (
        own,
        other,
        settled_one,
        settled_two,
        settled_near,
        raw,
        own_row,
        mate_row,
        flag_rows,
        spread_one,
        spread_two,
        by_frame,
        result,
        query_stack,
        ones_stack,
        usable,
        swap,
        weight_sem,
        own_sem,
        pair_send,
        pair_recv,
        spread_send,
        spread_recv,
        back_send,
        back_recv,
        raw_send,
        raw_recv,
        first_frame,
        visible,
        virtual_init,
        small_sem,
    ) = refs[5 + 2 * n_weights :]
    w_qkv, w_out, w_expand, w_shrink, w_cq = loaded[:5]
    late = loaded[5:]
    t = lax.axis_index("tracks")
    f = lax.axis_index("frames")
    group_index = lax.axis_index("groups")
    devices = n_tracks_axis * n_frames_axis
    me = t * n_frames_axis + f
    held, part, _ = tokens.shape
    mine = held // n_frames_axis
    length = part * n_frames_axis
    own_frames = length // devices
    all_tracks = held * n_tracks_axis
    virt = virtual_in.shape[0]
    pairs = (mine - SINGLE_TRACKS) // STEP_TRACKS
    late_pairs = pairs - EARLY_PAIRS
    blocks = own_frames // OCTET
    quarter = n_tracks_axis // 4
    half_devices = devices // 2
    zone = t // quarter
    is_inner = (zone + 1) // 2 % 2
    inner = is_inner == 1
    side_index = t // (n_tracks_axis // 2)
    mate_t = t + (1 - 2 * side_index) * quarter
    mate = mate_t * n_frames_axis + f

    def place(index):
        return (group_index, index // n_frames_axis, index % n_frames_axis)

    barrier = pltpu.get_barrier_semaphore()

    @pl.loop(1, devices, unroll=True)
    def _(k):
        pl.semaphore_signal(
            barrier,
            inc=1,
            device_id=place(lax.rem(me + k, devices)),
            device_id_type=MESH,
        )

    def own_copy(n):
        return pltpu.make_async_copy(tokens.at[f * mine + n], own.at[n], own_sem.at[n])

    loads = [
        pltpu.make_async_copy(stored[k], loaded[k], weight_sem.at[k]) for k in range(n_weights)
    ]
    small = [
        pltpu.make_async_copy(src, dst, small_sem.at[k])
        for k, (src, dst) in enumerate(
            ((first_frame_in, first_frame), (visible_in, visible), (virtual_in, virtual_init))
        )
    ]
    for copy in small:
        copy.start()
    own_copy(0).start()
    for load in loads[:4]:
        load.start()

    @pl.loop(1, mine)
    def _(n):
        own_copy(n).start()

    for load in loads[4:]:
        load.start()

    small[0].wait()
    small[1].wait()
    ids = lax.broadcasted_iota(jnp.int32, (1, length), 1)
    for n in range(held):
        started = first_frame[n]
        kept = (ids >= started) & ((visible[n : n + 1, :] == 1) | (ids == started))
        flag_rows[n : n + 1, :] = jnp.where(kept, 1.0, 0.0)
    usable[...] = jnp.transpose(flag_rows[...], (1, 0))
    row = flag_rows[pl.ds(f * mine + SHARED, 1), :]
    own_row[...] = jnp.where(f == 0, row, jnp.concatenate([row[:, part:], row[:, :part]], axis=1))
    for side in range(blocks):
        swap[side] = turn_matrix(side, mine, n_frames_axis, own_frames)
    for group in range(2):
        ones_stack[group] = jnp.concatenate(
            [
                jnp.where(head_mask(group, h, virt), 1.0, 0.0).astype(jnp.bfloat16)
                for h in range(GROUP)
            ],
            axis=0,
        )

    pl.semaphore_wait(barrier, devices - 1)

    def pair_copy(n):
        return pltpu.make_async_remote_copy(
            src_ref=tokens.at[(1 - f) * mine + n],
            dst_ref=other.at[n],
            send_sem=pair_send.at[n],
            recv_sem=pair_recv.at[n],
            device_id=(group_index, t, 1 - f),
            device_id_type=MESH,
        )

    def raw_copy(core):
        return pltpu.make_async_remote_copy(
            src_ref=tokens.at[core * mine + SHARED],
            dst_ref=raw.at[lax.rem(f + core, n_frames_axis)],
            send_sem=raw_send.at[0],
            recv_sem=raw_recv.at[0],
            device_id=(group_index, mate_t, core),
            device_id_type=MESH,
        )

    pair_copy(0).start()

    @pl.when(inner)
    def _():
        pltpu.make_async_remote_copy(
            src_ref=own_row,
            dst_ref=mate_row,
            send_sem=raw_send.at[1],
            recv_sem=raw_recv.at[1],
            device_id=(group_index, mate_t, f),
            device_id_type=MESH,
        ).start()
        for core in range(n_frames_axis):
            raw_copy(core).start()

    @pl.loop(1, mine)
    def _(n):
        pair_copy(n).start()

    def send(src, dst, sem, index):
        pltpu.make_async_remote_copy(
            src_ref=src,
            dst_ref=dst,
            send_sem=spread_send,
            recv_sem=spread_recv.at[sem],
            device_id=place(index),
            device_id_type=MESH,
        ).start()

    def base_of(index):
        return lax.rem(index + f, n_frames_axis) * part + (index // n_frames_axis) * own_frames

    def send_single(n, side):
        dst = spread_one.at[me, n]

        def source(index):
            at = pl.multiple_of(base_of(index), own_frames)
            return settled_one.at[n, pl.ds(at, own_frames), :]

        core = lax.rem(f + side, n_frames_axis)

        @pl.loop(0, n_tracks_axis - 1, unroll=True)
        def _(k):
            index = ordered(t, n_tracks_axis, k) * n_frames_axis + core
            send(source(index), dst, 0, index)

        if side == 0:
            pltpu.make_async_copy(source(me), dst, spread_recv.at[0]).start()
        else:
            index = t * n_frames_axis + core
            send(source(index), dst, 0, index)

    def send_pairs(p, count, block, n_blocks, sem):
        if n_blocks == blocks:
            dst = spread_two.at[me, p]
        else:
            dst = spread_two.at[me, pl.ds(p, count), block]

        def source(index):
            at = base_of(index) // OCTET + block
            if n_blocks == blocks:
                return settled_two.at[p, pl.ds(at, blocks)]
            return settled_two.at[pl.ds(p, count), at]

        @pl.loop(0, devices - 1, unroll=True)
        def _(k):
            index = ordered(me, devices, k)
            send(source(index), dst, sem, index)

        pltpu.make_async_copy(source(me), dst, spread_recv.at[sem]).start()

    lane = lax.broadcasted_iota(jnp.int32, (part, held), 1)

    def flags_of(n):
        chosen = lane == f * mine + n
        column = []
        for side in range(n_frames_axis):
            at = pl.multiple_of(lax.rem(f + side, n_frames_axis) * part, part)
            seen = jnp.where(chosen, usable[pl.ds(at, part), :], 0.0)
            column.append(jnp.sum(seen, axis=1, keepdims=True))
        return jnp.concatenate(column, axis=0)

    def gather(n):
        own_copy(n).wait()
        pair_copy(n).wait_recv()
        return [own[n], other[n]], flags_of(n)

    for load in loads[:4]:
        load.wait()

    @pl.loop(0, SINGLE_TRACKS - is_inner)
    def _(n):
        pieces, flags = gather(n)
        x = jnp.concatenate(pieces, axis=0).astype(jnp.float32)
        query, key, value = time_queries(x, w_qkv)
        mixed = time_attend(query, time_keys(key, value, flags))
        done = time_close(x, mixed, w_out, w_expand, w_shrink)
        settled_one[n] = done.astype(jnp.bfloat16)
        for side in range(n_frames_axis):
            send_single(n, side)

    span = part // 2

    def near(values):
        kept = []
        for core in range(n_frames_axis):
            low = values[core * part : core * part + span]
            high = values[core * part + span : (core + 1) * part]
            kept.append(jnp.where(side_index == 0, low, high))
        return jnp.concatenate(kept, axis=0)

    def near_source(k, index):
        at = lax.rem(index + f, n_frames_axis) * span
        at += (index // n_frames_axis - side_index * (n_tracks_axis // 2)) * own_frames
        return settled_near.at[k, pl.ds(pl.multiple_of(at, own_frames), own_frames), :]

    @pl.loop(0, pairs)
    def _(p):
        pieces, flags = [], []
        for k in range(STEP_TRACKS):
            piece, flag = gather(SINGLE_TRACKS + p * STEP_TRACKS + k)
            pieces += piece
            flags.append(flag)
        x = jnp.concatenate(pieces, axis=0).astype(jnp.float32)
        query, key, value = time_queries(x, w_qkv)
        mixed = []
        for k in range(STEP_TRACKS):
            rows = slice(k * length, (k + 1) * length)
            mixed.append(time_attend(query[rows], time_keys(key[rows], value[rows], flags[k])))
        done = time_close(x, jnp.concatenate(mixed, axis=0), w_out, w_expand, w_shrink)
        done = done.reshape(STEP_TRACKS, length // OCTET, OCTET, D)
        done = jnp.transpose(done, (1, 0, 2, 3)).reshape(length // OCTET, STEP_TRACKS * OCTET, D)
        settled_two[p] = done.astype(jnp.bfloat16)

        if EARLY_PAIRS:

            @pl.when(p < EARLY_PAIRS)
            def _():
                send_pairs(p, 1, 0, blocks, 1)

        @pl.when(p >= EARLY_PAIRS)
        def _():
            send_pairs(p, 1, 0, 1, 2)

    for block in range(1, blocks):
        send_pairs(EARLY_PAIRS, late_pairs, block, 1, 2 + block)

    @pl.when(inner)
    def _():
        pieces, flags = gather(SHARED)
        pltpu.make_async_copy(raw, raw, raw_recv.at[0]).wait()
        pltpu.make_async_copy(mate_row, mate_row, raw_recv.at[1]).wait()
        mate_flags = jnp.transpose(jnp.broadcast_to(mate_row[...], (OCTET, length)), (1, 0))
        flags = [flags, mate_flags[:, :1]]
        pieces += [raw[core] for core in range(n_frames_axis)]
        x = jnp.concatenate(pieces, axis=0).astype(jnp.float32)
        query, key, value = time_queries(x, w_qkv)
        mixed, kept = [], []
        for k in range(2):
            rows = slice(k * length, (k + 1) * length)
            keys = time_keys(key[rows], value[rows], flags[k])
            mixed.append(time_attend(near(query[rows]), keys))
            kept.append(near(x[rows]))
        mixed, kept = jnp.concatenate(mixed, axis=0), jnp.concatenate(kept, axis=0)
        done = time_close(kept, mixed, w_out, w_expand, w_shrink)
        settled_near[...] = done.astype(jnp.bfloat16).reshape(2, n_frames_axis * span, D)
        start = side_index * half_devices
        for k, owner in enumerate((me, mate)):
            dst = spread_one.at[owner, SHARED]

            @pl.loop(1, half_devices, unroll=True)
            def _(j):
                index = start + lax.rem(me - start + j, half_devices)
                send(near_source(k, index), dst, 0, index)

            pltpu.make_async_copy(near_source(k, me), dst, spread_recv.at[0]).start()

    for load in loads[4:]:
        load.wait()
    small[2].wait()
    virtual = virtual_init[...].astype(jnp.float32)
    virtual_query = unit(dot(unit(virtual).astype(jnp.bfloat16), w_cq[...])) * QSCALE
    for group in range(2):
        query_stack[group] = head_stack(virtual_query, group).astype(jnp.bfloat16)

    @pl.loop(0, mine)
    def _(n):
        pair_copy(n).wait_send()

    def arrived(ref, sem):
        pltpu.make_async_copy(ref, ref, spread_recv.at[sem]).wait()

    arrived(spread_one, 0)
    if EARLY_PAIRS:
        arrived(spread_two.at[:, pl.ds(0, EARLY_PAIRS)], 1)

    @pl.loop(0, blocks)
    def _(side):
        arrived(spread_two.at[:, pl.ds(EARLY_PAIRS, late_pairs), 0], 2 + side)
        at_frame = pl.multiple_of(side * OCTET, OCTET)

        @pl.loop(0, n_tracks_axis)
        def _(c):
            one = spread_one[pl.ds(c * n_frames_axis, n_frames_axis)]
            two = spread_two[pl.ds(c * n_frames_axis, n_frames_axis), :, side]
            rows = jnp.concatenate([one.reshape(-1, D), two.reshape(-1, D)], axis=0)
            turned = dot(swap[side], rows).astype(jnp.bfloat16)
            at = pl.multiple_of(c * held, held)
            by_frame[pl.ds(at_frame, OCTET), pl.ds(at, held), :] = turned.reshape(OCTET, held, D)

        @pl.loop(0, OCTET // STEP_FRAMES)
        def _(step):
            f0 = side * OCTET + step * STEP_FRAMES
            s = by_frame[pl.ds(f0, STEP_FRAMES)].reshape(STEP_FRAMES * all_tracks, D)
            done = frame_rows(
                s,
                query_stack,
                ones_stack,
                virtual_init[...].astype(jnp.float32),
                STEP_FRAMES,
                late,
            )
            result[pl.ds(f0, STEP_FRAMES)] = done.reshape(STEP_FRAMES, all_tracks, D)
            dst = returned.at[t, pl.ds(f0, STEP_FRAMES)]

            def source(index):
                return result.at[
                    pl.ds(f0, STEP_FRAMES), pl.ds(pl.multiple_of(index * held, held), held), :
                ]

            @pl.loop(0, n_tracks_axis - 1, unroll=True)
            def _(k):
                index = ordered(t, n_tracks_axis, k)
                pltpu.make_async_remote_copy(
                    src_ref=source(index),
                    dst_ref=dst,
                    send_sem=back_send,
                    recv_sem=back_recv,
                    device_id=(group_index, index, f),
                    device_id_type=MESH,
                ).start()

            pltpu.make_async_copy(source(t), dst, back_recv).start()

    others = length - own_frames
    sent = settled_one.at[pl.ds(0, SHARED), pl.ds(0, others), :]
    pltpu.make_async_copy(sent, sent, spread_send).wait()

    @pl.when(inner)
    def _():
        sent = settled_near.at[:, pl.ds(0, part - own_frames), :]
        pltpu.make_async_copy(sent, sent, spread_send).wait()
        pltpu.make_async_copy(raw, raw, raw_send.at[0]).wait()
        pltpu.make_async_copy(own_row, own_row, raw_send.at[1]).wait()

    @pl.when(is_inner == 0)
    def _():
        sent = settled_one.at[SHARED, pl.ds(0, others), :]
        pltpu.make_async_copy(sent, sent, spread_send).wait()

    sent = settled_two.at[:, pl.ds(0, others // OCTET)]
    pltpu.make_async_copy(sent, sent, spread_send).wait()
    sent = result.at[:, pl.ds(0, all_tracks - held), :]
    pltpu.make_async_copy(sent, sent, back_send).wait()
    pltpu.make_async_copy(returned, returned, back_recv).wait()


def fused_device(n_tracks_axis, n_frames_axis, tokens, first_frame, visible, *rest):
    (w_qkv, w_out, w_expand, w_shrink, virtual_init, w_cq, *late) = rest
    weights = (w_qkv, w_out, w_expand, w_shrink, w_cq, *late)
    held, part, _ = tokens.shape
    mine = held // n_frames_axis
    length = part * n_frames_axis
    devices = n_tracks_axis * n_frames_axis
    own_frames = length // devices
    all_tracks = held * n_tracks_axis
    pairs = (mine - SINGLE_TRACKS) // STEP_TRACKS
    unit_rows = STEP_TRACKS * OCTET
    blocks = own_frames // OCTET
    hbm = pl.BlockSpec(memory_space=pltpu.HBM)
    virt = virtual_init.shape[0]
    bf16 = jnp.bfloat16
    dma = pltpu.SemaphoreType.DMA
    turn_rows = n_frames_axis * (SINGLE_TRACKS * own_frames + pairs * unit_rows)
    returned = pl.pallas_call(
        functools.partial(layer_kernel, n_tracks_axis, n_frames_axis, len(weights)),
        out_shape=OUT((n_tracks_axis, own_frames, held, D), bf16),
        in_specs=[hbm] * (4 + len(weights)),
        out_specs=pl.BlockSpec(memory_space=OUT),
        scratch_shapes=[pltpu.VMEM(w.shape, w.dtype) for w in weights]
        + [
            pltpu.VMEM((mine, part, D), bf16),
            pltpu.VMEM((mine, part, D), bf16),
            pltpu.VMEM((SINGLE_TRACKS, length, D), bf16),
            pltpu.VMEM((pairs, length // OCTET, unit_rows, D), bf16),
            pltpu.VMEM((2, part, D), bf16),
            pltpu.VMEM((n_frames_axis, part, D), bf16),
            pltpu.VMEM((1, length), jnp.float32),
            pltpu.VMEM((1, length), jnp.float32),
            pltpu.VMEM((held, length), jnp.float32),
            pltpu.VMEM((devices, SINGLE_TRACKS, own_frames, D), bf16),
            pltpu.VMEM((devices, pairs, blocks, unit_rows, D), bf16),
            pltpu.VMEM((own_frames, all_tracks, D), bf16),
            pltpu.VMEM((own_frames, all_tracks, D), bf16),
            pltpu.VMEM((2, GROUP * virt, WIN), bf16),
            pltpu.VMEM((2, GROUP * virt, WIN), bf16),
            pltpu.VMEM((length, held), jnp.float32),
            pltpu.VMEM((blocks, OCTET * held, turn_rows), bf16),
            dma((len(weights),)),
            dma((mine,)),
            dma((mine,)),
            dma((mine,)),
            dma,
            dma((2 + blocks,)),
            dma,
            dma,
            dma((2,)),
            dma((2,)),
            pltpu.SMEM(first_frame.shape, first_frame.dtype),
            pltpu.VMEM(visible.shape, visible.dtype),
            pltpu.VMEM(virtual_init.shape, virtual_init.dtype),
            dma((3,)),
        ],
        compiler_params=pltpu.CompilerParams(
            collective_id=0, has_side_effects=True, vmem_limit_bytes=VMEM_BYTES
        ),
    )(tokens, first_frame, visible, virtual_init, *weights)
    return jnp.transpose(returned, (2, 0, 1, 3)).reshape(tokens.shape)


def fits(tracks_axis, frames_axis, tokens):
    held = tokens.shape[0]
    own_frames = tokens.shape[1] // tracks_axis
    mine = held // 2
    return (
        frames_axis == 2
        and tracks_axis % 4 == 0
        and mine > SINGLE_TRACKS
        and (mine - SINGLE_TRACKS) % STEP_TRACKS == 0
        and own_frames == held
        and own_frames == 2 * OCTET
        and STEP_TRACKS * OCTET == 16
        and tokens.shape[1] % 128 == 0
    )


def solution(mesh):
    placed = (
        P(("groups", "tracks"), "frames", None),
        P(("groups", "tracks")),
        P(("groups", "tracks"), None),
        P(),
        P(),
        P(),
        P(),
        P(),
        P(),
        P(),
        P(),
        P(),
        P(),
        P(),
        P(),
        P(),
    )
    axes = (mesh.shape["tracks"], mesh.shape["frames"])

    def body(tokens, *rest):
        if fits(*axes, tokens):
            return fused_device(*axes, tokens, *rest)
        return per_device(tokens, *rest)

    return jax.shard_map(
        body,
        mesh=mesh,
        in_specs=placed,
        out_specs=P(("groups", "tracks"), "frames", None),
        check_vma=False,
    )
```
